256 devices in a mesh: row: 8 (over x, core), col: 32 (over z, y).
Axes of the slice: x: 4, y: 4, z: 8, core: 2. Of those that a mesh axis runs over, the one named last changes fastest.
Arguments:
- momentum: float32 [5120, 27648], P('row', 'col'), may hold values from -130 to 130, as said below
- activations: bfloat16 [2048, 5120], P(None, 'row'), may hold values from -6 to 6
- out_grads: bfloat16 [2048, 27648], P(None, 'col'), may hold values from -0.125 to 0.125
- basis: float32 [27648, 256], P('col'), may hold values from -6 to 6
Outputs:
- new_momentum: float32 [5120, 27648], P('row', 'col')
- left_basis: float32 [5120, 256], P('row')
- new_basis: float32 [27648, 256], P('col')
The draws below stay inside these ranges and needn't reach their ends.
Inputs may be any that keep to these rules, and one draw needn't show every extreme that they name: `momentum`: Real-valued entries of order one with varying row and column scales.
All inputs are finite; a program needn't handle non-finite values.
Results may differ from the reference program's by a relative error of at most 0.0003.
Values sent between devices are 32-bit elements; how exact they have to be, the bound alone decides.
A program may use at most 128 MiB of HBM per device.

```python
import math
import jax
import jax.numpy as jnp
from jax import lax

D = 5120
F = 27648
RANK = 256
TOKENS = 2048


def draw_momentum(key, part):
    keys = jax.random.split(jax.random.fold_in(key, 11), 3)
    row_pos = jnp.arange(D, dtype=jnp.float32) / D
    col_pos = jnp.arange(F, dtype=jnp.float32) / F
    trend_rows = jnp.exp(0.5 * math.log(3.0) * (row_pos - 0.5))
    trend_cols = jnp.exp(0.5 * math.log(3.0) * (col_pos - 0.5))
    base = jax.random.truncated_normal(keys[0], -4.0, 4.0, (D, F), jnp.float32)
    row_scale = jnp.exp(jax.random.uniform(keys[1], (D,), jnp.float32, math.log(0.3), math.log(3.0))) * trend_rows
    col_scale = jnp.exp(jax.random.uniform(keys[2], (F,), jnp.float32, math.log(0.3), math.log(3.0))) * trend_cols
    return base * row_scale[:, None] * col_scale[None, :]


def shard_levels(rng, extent, pieces, low, high):
    gain, own = 1.0, jax.random.fold_in(rng, 6)
    for axis_at, shards_of in pieces:
        draws = jnp.exp(jax.random.uniform(jax.random.fold_in(own, axis_at), (shards_of,), jnp.float32, low / len(pieces), high / len(pieces)))
        gain = gain * jnp.repeat(draws, extent[axis_at] // shards_of).reshape([-1 if axis == axis_at else 1 for axis in range(len(extent))])
    return gain


def bell_draw(rng, dims, scale, most, cuts=(), kind=jnp.bfloat16):
    level = shard_levels(rng, dims, cuts, -0.22, 0.18) if cuts else 1.0
    array = jax.random.normal(rng, dims, jnp.float32) * scale * level
    return jnp.minimum(jnp.maximum(array, -most), most).astype(kind)


def setup_inputs(seed: int = 0) -> dict:
    seeds = jax.random.split(jax.random.key(seed), 5)
    momentum = draw_momentum(jax.random.fold_in(seeds[4], 71), 0)
    activations = bell_draw(seeds[1], (TOKENS, D), 1.0, 6.0, ((1, 8),))
    out_grads = bell_draw(seeds[2], (TOKENS, F), TOKENS ** -0.5, 0.125, ((1, 32),))
    basis = bell_draw(seeds[3], (F, RANK), 1.0, 6.0, ((0, 32),), jnp.float32)
    return dict(momentum=momentum, activations=activations, out_grads=out_grads, basis=basis)


EPS = 1e-06
HIGH = lax.Precision.HIGHEST

def reference(momentum, activations, out_grads, basis):
    gradient = lax.dot_general(activations.astype(jnp.float32), out_grads.astype(jnp.float32), (((0,), (0,)), ((), ())), preferred_element_type=jnp.float32)
    merged = momentum + gradient
    projected = jnp.dot(merged, basis, precision=HIGH)
    gram_total = jnp.dot(projected.T, projected, precision=HIGH)
    factor = jnp.linalg.cholesky(gram_total)
    ortho = jax.scipy.linalg.solve_triangular(factor, projected.T, lower=True).T
    coeffs = jnp.dot(merged.T, ortho, precision=HIGH)
    new_momentum = merged - 0.5 * jnp.dot(ortho, coeffs.T, precision=HIGH)
    inv_norm = lax.rsqrt(lax.optimization_barrier(jnp.mean(coeffs * coeffs, axis=0)) + EPS)
    return (new_momentum, ortho * jnp.float32(math.sqrt(D)), coeffs * inv_norm[None, :])
```

```python
import math

import jax
import jax.numpy as jnp
from jax import lax
from jax.experimental import pallas as pl
from jax.experimental.pallas import tpu as pltpu
from jax.sharding import PartitionSpec as P

D = 5120
F = 27648
EPS = 1e-06
HIGH = lax.Precision.HIGHEST
MESH = pl.DeviceIdType.MESH
F32 = jnp.float32
BF16 = jnp.bfloat16

XS, YS, ZS = 4, 4, 8
ROWS, COLS, RANK, TOKENS = 640, 864, 256, 2048
COLS_PAD = 896
STEP = 288
GROUPS = ((0, 2), (2, 2), (4, 1))


def mm(a, b, ca, cb):
    return lax.dot_general(a, b, (((ca,), (cb,)), ((), ())), precision=HIGH, preferred_element_type=F32)


def mm16(a, b, ca, cb):
    return lax.dot_general(a, b, (((ca,), (cb,)), ((), ())), preferred_element_type=F32)


def halves(x):
    hi = x.astype(BF16)
    return hi, (x - hi.astype(F32)).astype(BF16)


def mm3(a, b, ca, cb):
    return mm16(a[0], b[0], ca, cb) + (mm16(a[0], b[1], ca, cb) + mm16(a[1], b[0], ca, cb))


def lane_of(v, c):
    return jnp.broadcast_to(v[:, c:c + 1], v.shape)

def row_of(v, r):
    return jnp.broadcast_to(v[r:r + 1, :], v.shape)

def inverse_factor_64(block):
    r64 = lax.broadcasted_iota(jnp.int32, (64, 64), 0)
    c64 = lax.broadcasted_iota(jnp.int32, (64, 64), 1)
    eye = jnp.where(r64 == c64, 1.0, 0.0).astype(jnp.float32)
    wide = jnp.concatenate([block, eye], axis=1)
    t = [wide[8 * k:8 * k + 8] for k in range(8)]
    sub = lax.broadcasted_iota(jnp.int32, (8, 128), 0)
    out = []
    for k in range(8):
        cols = [lane_of(t[k], 8 * k + c) for c in range(8)]
        e = [[row_of(cols[c], r) if r >= c else None for c in range(8)] for r in range(8)]
        rows = [row_of(t[k], r) for r in range(8)]
        rs = [None] * 8
        l = [[None] * 8 for _ in range(8)]
        for c in range(8):
            rs[c] = lax.rsqrt(e[c][c])
            rows[c] = rows[c] * rs[c]
            for r in range(c + 1, 8):
                l[r][c] = e[r][c] * rs[c]
            for r in range(c + 1, 8):
                for m in range(c + 1, r + 1):
                    e[r][m] = e[r][m] - l[r][c] * l[m][c]
                rows[r] = rows[r] - l[r][c] * rows[c]
        u = rows[0]
        for c in range(1, 8):
            u = jnp.where(sub == c, rows[c], u)
        out.append(u)
        for j in range(k + 1, 8):
            s = [lane_of(t[j], 8 * k + c) for c in range(8)]
            for c in range(8):
                s[c] = s[c] * rs[c]
                for m in range(c + 1, 8):
                    s[m] = s[m] - s[c] * l[m][c]
                t[j] = t[j] - s[c] * rows[c]
    return jnp.concatenate(out, axis=0)[:, 64:]

def joined(w11, w21, w22):
    top = jnp.concatenate([w11, jnp.zeros_like(w11)], axis=1)
    return jnp.concatenate([top, jnp.concatenate([w21, w22], axis=1)], axis=0)

def inverse_factor_step(a11, a21, a22, smaller):
    w11 = smaller(a11)
    l21 = mm(a21, w11, 1, 1)
    s = a22 - mm(l21, l21, 1, 1)
    lw = mm(l21, w11, 1, 0)
    w22 = smaller(s)
    w21 = -mm(w22, lw, 1, 0)
    return w11, w21, w22

def inverse_factor_128(a):
    return joined(*inverse_factor_step(a[:64, :64], a[64:, :64], a[64:, 64:], inverse_factor_64))


def kernel(mom_hbm, act_hbm, grad_hbm, basis_hbm, newm_hbm, left_hbm, newb_hbm,
           grad, act, merged, basis, bt_hi, bt_lo, m_hi, m_lo,
           part, from_y, mine, from_z, full,
           gram, gram_pair, gram_x, gram_all,
           coef, coef_pair, coef_sum, coef_x, coef_all,
           right, r_hi, r_lo, left, sq_z, sq_y,
           send, recv, local):
    row, col = lax.axis_index("row"), lax.axis_index("col")
    x, core = row // 2, lax.rem(row, 2)
    z, y = col // YS, lax.rem(col, YS)

    def at_y(d):
        return (row, z * YS + lax.rem(y + d, YS))

    def at_z(d):
        return (row, lax.rem(z + d, ZS) * YS + y)

    def at_x(d):
        return (lax.rem(x + d, XS) * 2 + core, col)

    other = (x * 2 + 1 - core, col)

    loads = [
        pltpu.make_async_copy(act_hbm.at[:, pl.ds(128 * t, 128 * n)], act.at[:, pl.ds(128 * t, 128 * n)], local.at[i])
        for i, (t, n) in enumerate(GROUPS)
    ]
    grad_load = [
        pltpu.make_async_copy(grad_hbm.at[pl.ds(STEP * i, STEP)], grad.at[pl.ds(STEP * i, STEP)], local.at[3 + i])
        for i in range(3)
    ]
    mom_load = pltpu.make_async_copy(mom_hbm, merged, local.at[6])
    basis_load = pltpu.make_async_copy(basis_hbm, basis.at[pl.ds(0, COLS)], local.at[7])
    basis_load.start()
    loads[0].start()
    for c in grad_load:
        c.start()
    mom_load.start()
    loads[1].start()
    loads[2].start()

    barrier = pltpu.get_barrier_semaphore()
    peers = [at_y(d) for d in range(1, YS)] + [at_z(d) for d in range(1, ZS)] + [at_x(d) for d in range(1, XS)] + [other]
    for peer in peers:
        pl.semaphore_signal(barrier, inc=1, device_id=peer, device_id_type=MESH)

    count = [0]
    started = []

    def remote(src, dst, peer):
        n = count[0]
        count[0] += 1
        copy = pltpu.make_async_remote_copy(
            src_ref=src, dst_ref=dst, send_sem=send.at[n], recv_sem=recv.at[n], device_id=peer, device_id_type=MESH)
        copy.start()
        started.append(copy)
        return copy

    basis[COLS:, :] = jnp.zeros((COLS_PAD - COLS, RANK), F32)
    m_hi[COLS:, :] = jnp.zeros((COLS_PAD - COLS, ROWS), BF16)
    m_lo[COLS:, :] = jnp.zeros((COLS_PAD - COLS, ROWS), BF16)
    basis_load.wait()
    for i in range(COLS_PAD // 128):
        hi, lo = halves(basis[128 * i:128 * i + 128, :].T)
        bt_hi[:, 128 * i:128 * i + 128] = hi
        bt_lo[:, 128 * i:128 * i + 128] = lo

    def project(g):
        t, n = GROUPS[g]
        lanes = slice(128 * t, 128 * (t + n))
        loads[g].wait()
        if g == 0:
            for c in grad_load:
                c.wait()
            mom_load.wait()

        @pl.loop(0, COLS // STEP)
        def _(i):
            rows = pl.ds(pl.multiple_of(i * STEP, STEP), STEP)
            m = merged[rows, lanes] + mm16(grad[rows, :], act[:, lanes], 1, 0)
            merged[rows, lanes] = m
            hi, lo = halves(m)
            m_hi[rows, lanes] = hi
            m_lo[rows, lanes] = lo

        p = mm3((bt_hi[...], bt_lo[...]), (m_hi[:, lanes], m_lo[:, lanes]), 1, 0)
        for k in range(n):
            part[t + k] = p[:, 128 * k:128 * k + 128]

    def span(g):
        return pl.ds(*GROUPS[g])

    def mine_y(d):
        return pl.ds(pl.multiple_of(64 * lax.rem(y + d, YS), 64), 64)

    def mine_z(d):
        return pl.ds(pl.multiple_of(8 * lax.rem(z + d, ZS), 8), 8)

    own = pl.ds(pl.multiple_of(64 * y + 8 * z, 8), 8)

    def scatter_y(g):
        return [remote(part.at[span(g), mine_y(d)], from_y.at[d - 1, span(g)], at_y(d)) for d in range(1, YS)]

    def scatter_z(g, before):
        for c in before:
            c.wait_recv()
        t, n = GROUPS[g]
        for k in range(t, t + n):
            mine[k] = (part[k, mine_y(0), :] + from_y[0, k]) + (from_y[1, k] + from_y[2, k])
        return [remote(mine.at[span(g), mine_z(d)], from_z.at[d - 1, span(g)], at_z(d)) for d in range(1, ZS)]

    def gather_z(g, before):
        for c in before:
            c.wait_recv()
        t, n = GROUPS[g]
        for k in range(t, t + n):
            total = mine[k, mine_z(0), :]
            for d in range(ZS - 1):
                total = total + from_z[d, k]
            full[k, own, :] = total
        return [remote(full.at[span(g), own], full.at[span(g), own], at_z(d)) for d in range(1, ZS)]

    def gather_y(g, before):
        for c in before:
            c.wait_recv()
        return [remote(full.at[span(g), mine_y(0)], full.at[span(g), mine_y(0)], at_y(d)) for d in range(1, YS)]

    def whole(g):
        t, n = GROUPS[g]
        return jnp.concatenate([full[k] for k in range(t, t + n)], axis=1)

    def coefficients(g):
        t, n = GROUPS[g]
        lanes = slice(128 * t, 128 * (t + n))
        p = halves(whole(g))

        @pl.loop(0, COLS // STEP)
        def _(i):
            rows = pl.ds(pl.multiple_of(i * STEP, STEP), STEP)
            c = mm3((m_hi[rows, lanes], m_lo[rows, lanes]), p, 1, 1)
            for k in range(2):
                v = c[:, 128 * k:128 * k + 128]
                coef[k, rows, :] = v if g == 0 else coef[k, rows, :] + v

    project(0)
    pl.semaphore_wait(barrier, len(peers))
    a0 = scatter_y(0)
    project(1)
    a1 = scatter_y(1)
    b0 = scatter_z(0, a0)
    project(2)
    a2 = scatter_y(2)
    b1 = scatter_z(1, a1)
    c0 = gather_z(0, b0)
    b2 = scatter_z(2, a2)
    c1 = gather_z(1, b1)
    d0 = gather_y(0, c0)
    c2 = gather_z(2, b2)
    d1 = gather_y(1, c1)
    d2 = gather_y(2, c2)
    for c in d0:
        c.wait_recv()
    gr = mm(whole(0), whole(0), 1, 1)
    coefficients(0)
    for c in d1:
        c.wait_recv()
    gr = gr + mm(whole(1), whole(1), 1, 1)
    coefficients(1)
    for c in d2:
        c.wait_recv()
    gr = gr + mm(whole(2), whole(2), 1, 1)

    gram[0] = gr[:128, :128]
    gram[1] = gr[128:, :128]
    gram[2] = gr[128:, 128:]
    half = pl.ds(pl.multiple_of(64 * core, 64), 64)
    other_half = pl.ds(pl.multiple_of(64 * (1 - core), 64), 64)
    e0 = remote(gram.at[pl.ds(0, 1), other_half], gram_pair.at[pl.ds(0, 1)], other)
    e1 = remote(gram.at[pl.ds(1, 2), other_half], gram_pair.at[pl.ds(1, 2)], other)
    coefficients(2)
    h = remote(coef.at[1 - core], coef_pair, other)

    def gram_over_x(b, n, before):
        before.wait_recv()
        for k in range(b, b + n):
            gram_x[x, k] = gram[k, half, :] + gram_pair[k]
        return [remote(gram_x.at[x, pl.ds(b, n)], gram_x.at[x, pl.ds(b, n)], at_x(d)) for d in range(1, XS)]

    def gram_to_pair(b, n, before):
        for c in before:
            c.wait_recv()
        for k in range(b, b + n):
            gram_all[k, half, :] = (gram_x[0, k] + gram_x[1, k]) + (gram_x[2, k] + gram_x[3, k])
        return remote(gram_all.at[pl.ds(b, n), half], gram_all.at[pl.ds(b, n), half], other)

    f0 = gram_over_x(0, 1, e0)
    f1 = gram_over_x(1, 2, e1)

    def coef_rows(d):
        return pl.ds(pl.multiple_of(216 * lax.rem(x + d, XS), 216), 216)

    h.wait_recv()
    coef_sum[...] = coef[core] + coef_pair[...]
    r = [remote(coef_sum.at[coef_rows(d)], coef_x.at[d - 1], at_x(d)) for d in range(1, XS)]
    g0 = gram_to_pair(0, 1, f0)
    g0.wait_recv()
    a11 = gram_all[0]
    w11 = inverse_factor_64(a11[:64, :64])
    l21 = mm(a11[64:, :64], w11, 1, 1)
    s = a11[64:, 64:] - mm(l21, l21, 1, 1)
    lw = mm(l21, w11, 1, 0)
    g1 = gram_to_pair(1, 2, f1)
    w22 = inverse_factor_64(s)
    wa = joined(w11, -mm(w22, lw, 1, 0), w22)
    g1.wait_recv()
    a22 = gram_all[2]
    l21 = mm(gram_all[1], wa, 1, 1)
    s = a22 - mm(l21, l21, 1, 1)
    lwa = mm(l21, wa, 1, 0)
    for c in r:
        c.wait_recv()
    coef_all[core, coef_rows(0), :] = (coef_sum[coef_rows(0), :] + coef_x[0]) + (coef_x[1] + coef_x[2])
    q = [remote(coef_all.at[core, coef_rows(0)], coef_all.at[core, coef_rows(0)], at_x(d)) for d in range(1, XS)]
    w11 = inverse_factor_64(s[:64, :64])
    l21 = mm(s[64:, :64], w11, 1, 1)
    s2 = s[64:, 64:] - mm(l21, l21, 1, 1)
    lw = mm(l21, w11, 1, 0)
    for c in q:
        c.wait_recv()
    k0 = remote(coef_all.at[core], coef_all.at[core], other)
    w22 = inverse_factor_64(s2)
    wb = joined(w11, -mm(w22, lw, 1, 0), w22)
    w = joined(wa, -mm(wb, lwa, 1, 0), wb)

    k0.wait_recv()
    w_parts = halves(w)

    def finish(i, squares):
        rows = pl.ds(pl.multiple_of(i * STEP, STEP), STEP)
        c = jnp.concatenate([coef_all[0, rows, :], coef_all[1, rows, :]], axis=1)
        c = mm3(halves(c), w_parts, 1, 1)
        right[rows, :] = c
        hi, lo = halves(c)
        r_hi[rows, :] = hi
        r_lo[rows, :] = lo
        return squares + jnp.sum(c * c, axis=0, keepdims=True)

    squares = lax.fori_loop(0, COLS // STEP, finish, jnp.zeros((1, RANK), F32))
    sq_z[z] = squares
    n = [remote(sq_z.at[z], sq_z.at[z], at_z(d)) for d in range(1, ZS)]

    outs = []
    for g, (t, num) in enumerate(GROUPS):
        lanes = slice(128 * t, 128 * (t + num))
        ortho = mm3(w_parts, halves(whole(g)), 1, 0)
        left[lanes, :] = (ortho * F32(math.sqrt(D))).T
        o = halves(ortho)

        @pl.loop(0, COLS // STEP)
        def _(i):
            rows = pl.ds(pl.multiple_of(i * STEP, STEP), STEP)
            merged[rows, lanes] = merged[rows, lanes] - 0.5 * mm3((r_hi[rows, :], r_lo[rows, :]), o, 1, 0)

        if g == 1:
            for c in n:
                c.wait_recv()
            total = sq_z[0]
            for k in range(1, ZS):
                total = total + sq_z[k]
            sq_y[y] = total
            v = [remote(sq_y.at[y], sq_y.at[y], at_y(d)) for d in range(1, YS)]
        out = pltpu.make_async_copy(merged.at[:, lanes], newm_hbm.at[:, lanes], local.at[8 + g])
        out.start()
        outs.append(out)
    out = pltpu.make_async_copy(left, left_hbm, local.at[11])
    out.start()
    outs.append(out)
    for c in v:
        c.wait_recv()
    total = (sq_y[0] + sq_y[1]) + (sq_y[2] + sq_y[3])
    inv = lax.rsqrt(total / F + EPS)
    right[...] = right[...] * inv
    out = pltpu.make_async_copy(right, newb_hbm, local.at[12])
    out.start()
    outs.append(out)
    for c in started:
        c.wait_send()
    for out in outs:
        out.wait()


COPIES = 3 * 20 + 10 + 8 + 10


def shards(momentum, activations, out_grads, basis):
    any_ = pl.BlockSpec(memory_space=pl.ANY)
    new_t, left, right = pl.pallas_call(
        kernel,
        out_shape=(
            jax.ShapeDtypeStruct((COLS, ROWS), F32),
            jax.ShapeDtypeStruct((ROWS, RANK), F32),
            jax.ShapeDtypeStruct((COLS, RANK), F32),
        ),
        in_specs=[any_] * 4,
        out_specs=[any_] * 3,
        scratch_shapes=[
            pltpu.VMEM((COLS, TOKENS), BF16),
            pltpu.VMEM((TOKENS, ROWS), BF16),
            pltpu.VMEM((COLS, ROWS), F32),
            pltpu.VMEM((COLS_PAD, RANK), F32),
            pltpu.VMEM((RANK, COLS_PAD), BF16),
            pltpu.VMEM((RANK, COLS_PAD), BF16),
            pltpu.VMEM((COLS_PAD, ROWS), BF16),
            pltpu.VMEM((COLS_PAD, ROWS), BF16),
            pltpu.VMEM((5, RANK, 128), F32),
            pltpu.VMEM((YS - 1, 5, 64, 128), F32),
            pltpu.VMEM((5, 64, 128), F32),
            pltpu.VMEM((ZS - 1, 5, 8, 128), F32),
            pltpu.VMEM((5, RANK, 128), F32),
            pltpu.VMEM((3, 128, 128), F32),
            pltpu.VMEM((3, 64, 128), F32),
            pltpu.VMEM((XS, 3, 64, 128), F32),
            pltpu.VMEM((3, 128, 128), F32),
            pltpu.VMEM((2, COLS, 128), F32),
            pltpu.VMEM((COLS, 128), F32),
            pltpu.VMEM((COLS, 128), F32),
            pltpu.VMEM((XS - 1, 216, 128), F32),
            pltpu.VMEM((2, COLS, 128), F32),
            pltpu.VMEM((COLS, RANK), F32),
            pltpu.VMEM((COLS, RANK), BF16),
            pltpu.VMEM((COLS, RANK), BF16),
            pltpu.VMEM((ROWS, RANK), F32),
            pltpu.VMEM((ZS, 1, RANK), F32),
            pltpu.VMEM((YS, 1, RANK), F32),
            pltpu.SemaphoreType.DMA((COPIES,)),
            pltpu.SemaphoreType.DMA((COPIES,)),
            pltpu.SemaphoreType.DMA((13,)),
        ],
        compiler_params=pltpu.CompilerParams(
            collective_id=0, has_side_effects=True, vmem_limit_bytes=48 * 1024 * 1024),
    )(momentum.T, activations, out_grads.T, basis)
    return new_t.T, left, right


def solution(mesh):
    return jax.shard_map(
        shards,
        mesh=mesh,
        in_specs=(P("row", "col"), P(None, "row"), P(None, "col"), P("col", None)),
        out_specs=(P("row", "col"), P("row", None), P("col", None)),
        check_vma=False,
    )
```

```python
import math

import jax
import jax.numpy as jnp
from jax import lax
from jax.experimental import pallas as pl
from jax.experimental.pallas import tpu as pltpu
from jax.sharding import PartitionSpec as P

D = 5120
F = 27648
EPS = 1e-06
HIGH = lax.Precision.HIGHEST
MESH = pl.DeviceIdType.MESH
F32 = jnp.float32
BF16 = jnp.bfloat16

XS, YS, ZS = 4, 4, 8
ROWS, COLS, RANK, TOKENS = 640, 864, 256, 2048
COLS_PAD = 896
STEP = 288
GROUPS = ((0, 2), (2, 2), (4, 1))
FAR_Z = (4, 3, 5, 2, 6, 1, 7)


def mm(a, b, ca, cb):
    return lax.dot_general(a, b, (((ca,), (cb,)), ((), ())), precision=HIGH, preferred_element_type=F32)


def mm16(a, b, ca, cb):
    return lax.dot_general(a, b, (((ca,), (cb,)), ((), ())), preferred_element_type=F32)


def halves(x):
    hi = x.astype(BF16)
    return hi, (x - hi.astype(F32)).astype(BF16)


def mm3(a, b, ca, cb):
    return mm16(a[0], b[0], ca, cb) + (mm16(a[0], b[1], ca, cb) + mm16(a[1], b[0], ca, cb))


def lane_of(v, c):
    return jnp.broadcast_to(v[:, c:c + 1], v.shape)

def row_of(v, r):
    return jnp.broadcast_to(v[r:r + 1, :], v.shape)

def inverse_factor_64(block):
    r64 = lax.broadcasted_iota(jnp.int32, (64, 64), 0)
    c64 = lax.broadcasted_iota(jnp.int32, (64, 64), 1)
    eye = jnp.where(r64 == c64, 1.0, 0.0).astype(jnp.float32)
    wide = jnp.concatenate([block, eye], axis=1)
    t = [wide[8 * k:8 * k + 8] for k in range(8)]
    sub = lax.broadcasted_iota(jnp.int32, (8, 128), 0)
    out = []
    for k in range(8):
        cols = [lane_of(t[k], 8 * k + c) for c in range(8)]
        e = [[row_of(cols[c], r) if r >= c else None for c in range(8)] for r in range(8)]
        rows = [row_of(t[k], r) for r in range(8)]
        rs = [None] * 8
        l = [[None] * 8 for _ in range(8)]
        for c in range(8):
            rs[c] = lax.rsqrt(e[c][c])
            rows[c] = rows[c] * rs[c]
            for r in range(c + 1, 8):
                l[r][c] = e[r][c] * rs[c]
            for r in range(c + 1, 8):
                for m in range(c + 1, r + 1):
                    e[r][m] = e[r][m] - l[r][c] * l[m][c]
                rows[r] = rows[r] - l[r][c] * rows[c]
        u = rows[0]
        for c in range(1, 8):
            u = jnp.where(sub == c, rows[c], u)
        out.append(u)
        for j in range(k + 1, 8):
            s = [lane_of(t[j], 8 * k + c) for c in range(8)]
            for c in range(8):
                s[c] = s[c] * rs[c]
                for m in range(c + 1, 8):
                    s[m] = s[m] - s[c] * l[m][c]
                t[j] = t[j] - s[c] * rows[c]
    return jnp.concatenate(out, axis=0)[:, 64:]

def joined(w11, w21, w22):
    top = jnp.concatenate([w11, jnp.zeros_like(w11)], axis=1)
    return jnp.concatenate([top, jnp.concatenate([w21, w22], axis=1)], axis=0)

def inverse_factor_step(a11, a21, a22, smaller):
    w11 = smaller(a11)
    l21 = mm(a21, w11, 1, 1)
    s = a22 - mm(l21, l21, 1, 1)
    lw = mm(l21, w11, 1, 0)
    w22 = smaller(s)
    w21 = -mm(w22, lw, 1, 0)
    return w11, w21, w22

def inverse_factor_128(a):
    return joined(*inverse_factor_step(a[:64, :64], a[64:, :64], a[64:, 64:], inverse_factor_64))


def kernel(mom_hbm, act_hbm, grad_hbm, basis_hbm, newm_hbm, left_hbm, newb_hbm, inv_hbm,
           grad, act, merged, basis, bt_hi, bt_lo, m_hi, m_lo,
           part, pass_y, sum_y, from_y, mine, from_z, full,
           gram, gram_pair, gram_x, gram_all,
           coef, coef_pair, coef_sum, coef_mid, coef_x, coef_all,
           right, r_hi, r_lo, left, sq_z, sq_y, inv,
           send, recv, local):
    row, col = lax.axis_index("row"), lax.axis_index("col")
    x, core = row // 2, lax.rem(row, 2)
    z, y = col // YS, lax.rem(col, YS)

    def at_y(d):
        return (row, z * YS + lax.rem(y + d, YS))

    def at_z(d):
        return (row, lax.rem(z + d, ZS) * YS + y)

    def at_x(d):
        return (lax.rem(x + d, XS) * 2 + core, col)

    other = (x * 2 + 1 - core, col)

    loads = [
        pltpu.make_async_copy(act_hbm.at[:, pl.ds(128 * t, 128 * n)], act.at[:, pl.ds(128 * t, 128 * n)], local.at[i])
        for i, (t, n) in enumerate(GROUPS)
    ]
    grad_load = [
        pltpu.make_async_copy(grad_hbm.at[pl.ds(STEP * i, STEP)], grad.at[pl.ds(STEP * i, STEP)], local.at[3 + i])
        for i in range(3)
    ]
    mom_load = [
        pltpu.make_async_copy(mom_hbm.at[pl.ds(STEP * i, STEP)], merged.at[pl.ds(STEP * i, STEP)], local.at[8 + i])
        for i in range(3)
    ]
    basis_load = pltpu.make_async_copy(basis_hbm, basis.at[pl.ds(0, COLS)], local.at[7])
    basis_load.start()
    loads[0].start()
    for i in range(3):
        grad_load[i].start()
        mom_load[i].start()
    loads[1].start()
    loads[2].start()

    barrier = pltpu.get_barrier_semaphore()
    peers = [at_y(d) for d in range(1, YS)] + [at_z(d) for d in range(1, ZS)] + [at_x(d) for d in range(1, XS)] + [other]
    for peer in peers:
        pl.semaphore_signal(barrier, inc=1, device_id=peer, device_id_type=MESH)

    count = [0]
    started = []

    def remote(src, dst, peer):
        n = count[0]
        count[0] += 1
        copy = pltpu.make_async_remote_copy(
            src_ref=src, dst_ref=dst, send_sem=send.at[n], recv_sem=recv.at[n], device_id=peer, device_id_type=MESH)
        copy.start()
        started.append(copy)
        return copy

    basis[COLS:, :] = jnp.zeros((COLS_PAD - COLS, RANK), F32)
    m_hi[COLS:, :] = jnp.zeros((COLS_PAD - COLS, ROWS), BF16)
    m_lo[COLS:, :] = jnp.zeros((COLS_PAD - COLS, ROWS), BF16)
    basis_load.wait()
    for i in range(COLS_PAD // 128):
        hi, lo = halves(basis[128 * i:128 * i + 128, :].T)
        bt_hi[:, 128 * i:128 * i + 128] = hi
        bt_lo[:, 128 * i:128 * i + 128] = lo

    def project(g):
        t, n = GROUPS[g]
        lanes = slice(128 * t, 128 * (t + n))
        loads[g].wait()

        def merge(i):
            rows = pl.ds(pl.multiple_of(i * STEP, STEP), STEP)
            m = merged[rows, lanes] + mm16(grad[rows, :], act[:, lanes], 1, 0)
            merged[rows, lanes] = m
            hi, lo = halves(m)
            m_hi[rows, lanes] = hi
            m_lo[rows, lanes] = lo

        if g == 0:
            for i in range(COLS // STEP):
                grad_load[i].wait()
                mom_load[i].wait()
                merge(i)
        else:
            pl.loop(0, COLS // STEP)(merge)

        p = mm3((bt_hi[...], bt_lo[...]), (m_hi[:, lanes], m_lo[:, lanes]), 1, 0)
        for k in range(n):
            part[t + k] = p[:, 128 * k:128 * k + 128]

    def span(g):
        return pl.ds(*GROUPS[g])

    def mine_y(d):
        return pl.ds(pl.multiple_of(64 * lax.rem(y + d, YS), 64), 64)

    def mine_z(d):
        return pl.ds(pl.multiple_of(8 * lax.rem(z + d, ZS), 8), 8)

    own = pl.ds(pl.multiple_of(64 * y + 8 * z, 8), 8)

    def rows_of(d, at, n):
        return pl.ds(pl.multiple_of(64 * lax.rem(y + d, YS) + at, 32), n)

    def scatter_y(g):
        t = span(g)
        return [
            remote(part.at[t, rows_of(2, 0, 32)], pass_y.at[0, t], at_y(1)),
            remote(part.at[t, rows_of(2, 32, 32)], pass_y.at[1, t], at_y(3)),
            remote(part.at[t, rows_of(1, 32, 32)], from_y.at[0, t, pl.ds(32, 32)], at_y(1)),
            remote(part.at[t, rows_of(3, 0, 32)], from_y.at[1, t, pl.ds(0, 32)], at_y(3)),
        ]

    def relay_y(g, before):
        t, n = GROUPS[g]
        after = before[2:]
        for way, (d, at) in enumerate(((1, 0), (3, 32))):
            before[way].wait_recv()
            for k in range(t, t + n):
                sum_y[way, k] = part[k, rows_of(d, at, 32), :] + pass_y[way, k]
            after.append(remote(sum_y.at[way, span(g)], from_y.at[way, span(g), pl.ds(at, 32)], at_y(d)))
        return after

    def scatter_z(g, before):
        for c in before:
            c.wait_recv()
        t, n = GROUPS[g]
        for k in range(t, t + n):
            mine[k] = (part[k, mine_y(0), :] + from_y[0, k]) + from_y[1, k]
        return [remote(mine.at[span(g), mine_z(d)], from_z.at[d - 1, span(g)], at_z(d)) for d in FAR_Z]

    def gather_z(g, before):
        for c in before:
            c.wait_recv()
        t, n = GROUPS[g]
        for k in range(t, t + n):
            total = mine[k, mine_z(0), :]
            for d in range(ZS - 1):
                total = total + from_z[d, k]
            full[k, own, :] = total
        return [remote(full.at[span(g), own], full.at[span(g), own], at_z(d)) for d in FAR_Z]

    def gather_y(g, before):
        for c in before:
            c.wait_recv()
        return [remote(full.at[span(g), mine_y(0)], full.at[span(g), mine_y(0)], at_y(d)) for d in (1, 3)]

    def pass_on_y(g, before):
        after = []
        for c, (source, to, at) in zip(before, ((3, 1, 0), (1, 3, 32))):
            c.wait_recv()
            block = full.at[span(g), rows_of(source, at, 32)]
            after.append(remote(block, block, at_y(to)))
        return after

    def whole(g):
        t, n = GROUPS[g]
        return jnp.concatenate([full[k] for k in range(t, t + n)], axis=1)

    def coefficients(g):
        t, n = GROUPS[g]
        lanes = slice(128 * t, 128 * (t + n))
        p = halves(whole(g))

        @pl.loop(0, COLS // STEP)
        def _(i):
            rows = pl.ds(pl.multiple_of(i * STEP, STEP), STEP)
            c = mm3((m_hi[rows, lanes], m_lo[rows, lanes]), p, 1, 1)
            for k in range(2):
                v = c[:, 128 * k:128 * k + 128]
                coef[k, rows, :] = v if g == 0 else coef[k, rows, :] + v

    project(0)
    pl.semaphore_wait(barrier, len(peers))
    a0 = scatter_y(0)
    project(1)
    a1 = scatter_y(1)
    a0 = relay_y(0, a0)
    project(2)
    a2 = scatter_y(2)
    b0 = scatter_z(0, a0)
    a1 = relay_y(1, a1)
    a2 = relay_y(2, a2)
    c0 = gather_z(0, b0)
    b1 = scatter_z(1, a1)
    b2 = scatter_z(2, a2)
    d0 = gather_y(0, c0)
    c1 = gather_z(1, b1)
    c2 = gather_z(2, b2)
    d0 = pass_on_y(0, d0)
    d1 = gather_y(1, c1)
    d2 = gather_y(2, c2)
    d1 = pass_on_y(1, d1)
    for c in d0:
        c.wait_recv()
    gr = mm(whole(0), whole(0), 1, 1)
    d2 = pass_on_y(2, d2)
    coefficients(0)
    for c in d1:
        c.wait_recv()
    gr = gr + mm(whole(1), whole(1), 1, 1)
    coefficients(1)
    for c in d2:
        c.wait_recv()
    gr = gr + mm(whole(2), whole(2), 1, 1)

    gram[0] = gr[:128, :128]
    gram[1] = gr[128:, :128]
    gram[2] = gr[128:, 128:]
    half = pl.ds(pl.multiple_of(64 * core, 64), 64)
    other_half = pl.ds(pl.multiple_of(64 * (1 - core), 64), 64)
    e0 = remote(gram.at[pl.ds(0, 1), other_half], gram_pair.at[pl.ds(0, 1)], other)
    e1 = remote(gram.at[pl.ds(1, 2), other_half], gram_pair.at[pl.ds(1, 2)], other)
    coefficients(2)
    h = remote(coef.at[1 - core], coef_pair, other)

    def gram_over_x(b, n, before):
        before.wait_recv()
        for k in range(b, b + n):
            gram_x[x, k] = gram[k, half, :] + gram_pair[k]
        return [remote(gram_x.at[x, pl.ds(b, n)], gram_x.at[x, pl.ds(b, n)], at_x(d)) for d in (1, 3)]

    def gram_pass_on(b, n, before):
        after = []
        for c, (source, to, at) in zip(before, ((3, 1, 0), (1, 3, 32))):
            c.wait_recv()
            block = gram_x.at[lax.rem(x + source, XS), pl.ds(b, n), pl.ds(at, 32)]
            after.append(remote(block, block, at_x(to)))
        return after

    def gram_to_pair(b, n, before):
        for c in before:
            c.wait_recv()
        for k in range(b, b + n):
            gram_all[k, half, :] = (gram_x[0, k] + gram_x[1, k]) + (gram_x[2, k] + gram_x[3, k])
        return remote(gram_all.at[pl.ds(b, n), half], gram_all.at[pl.ds(b, n), half], other)

    f0 = gram_over_x(0, 1, e0)
    f1 = gram_over_x(1, 2, e1)

    def coef_rows(d, at=0, n=216):
        return pl.ds(pl.multiple_of(216 * lax.rem(x + d, XS) + at, 8), n)

    def coef_to(d, block):
        return remote(coef_all.at[core, block], coef_all.at[core, block], d)

    f0 = gram_pass_on(0, 1, f0)
    h.wait_recv()
    coef_sum[...] = coef[core] + coef_pair[...]
    r_pass = [
        remote(coef_sum.at[coef_rows(2, 0, 112)], coef_x.at[2, pl.ds(0, 112)], at_x(1)),
        remote(coef_sum.at[coef_rows(2, 112, 104)], coef_x.at[3, pl.ds(0, 104)], at_x(3)),
    ]
    r = [
        remote(coef_sum.at[coef_rows(1, 112, 104)], coef_x.at[0, pl.ds(112, 104)], at_x(1)),
        remote(coef_sum.at[coef_rows(3, 0, 112)], coef_x.at[1, pl.ds(0, 112)], at_x(3)),
    ]
    g0 = gram_to_pair(0, 1, f0)
    f1 = gram_pass_on(1, 2, f1)
    g0.wait_recv()
    a11 = gram_all[0]
    w11 = inverse_factor_64(a11[:64, :64])
    l21 = mm(a11[64:, :64], w11, 1, 1)
    s = a11[64:, 64:] - mm(l21, l21, 1, 1)
    lw = mm(l21, w11, 1, 0)
    g1 = gram_to_pair(1, 2, f1)
    r_pass[0].wait_recv()
    coef_mid[0:112] = coef_sum[coef_rows(1, 0, 112), :] + coef_x[2, 0:112]
    r.append(remote(coef_mid.at[pl.ds(0, 112)], coef_x.at[0, pl.ds(0, 112)], at_x(1)))
    r_pass[1].wait_recv()
    coef_mid[112:216] = coef_sum[coef_rows(3, 112, 104), :] + coef_x[3, 0:104]
    r.append(remote(coef_mid.at[pl.ds(112, 104)], coef_x.at[1, pl.ds(112, 104)], at_x(3)))
    w22 = inverse_factor_64(s)
    wa = joined(w11, -mm(w22, lw, 1, 0), w22)
    g1.wait_recv()
    a22 = gram_all[2]
    l21 = mm(gram_all[1], wa, 1, 1)
    s = a22 - mm(l21, l21, 1, 1)
    lwa = mm(l21, wa, 1, 0)
    for c in r:
        c.wait_recv()
    coef_all[core, coef_rows(0), :] = (coef_sum[coef_rows(0), :] + coef_x[0]) + coef_x[1]
    q = [coef_to(at_x(1), coef_rows(0)), coef_to(at_x(3), coef_rows(0))]
    k = [coef_to(other, coef_rows(0))]
    w11 = inverse_factor_64(s[:64, :64])
    l21 = mm(s[64:, :64], w11, 1, 1)
    s2 = s[64:, 64:] - mm(l21, l21, 1, 1)
    lw = mm(l21, w11, 1, 0)
    q[0].wait_recv()
    q.append(coef_to(at_x(1), coef_rows(3, 0, 112)))
    k.append(coef_to(other, coef_rows(3)))
    q[1].wait_recv()
    q.append(coef_to(at_x(3), coef_rows(1, 112, 104)))
    k.append(coef_to(other, coef_rows(1)))
    w22 = inverse_factor_64(s2)
    wb = joined(w11, -mm(w22, lw, 1, 0), w22)
    w = joined(wa, -mm(wb, lwa, 1, 0), wb)
    q[2].wait_recv()
    q[3].wait_recv()
    k.append(coef_to(other, coef_rows(2)))

    for c in k:
        c.wait_recv()
    w_parts = halves(w)

    def finish(i, squares):
        rows = pl.ds(pl.multiple_of(i * STEP, STEP), STEP)
        c = jnp.concatenate([coef_all[0, rows, :], coef_all[1, rows, :]], axis=1)
        c = mm3(halves(c), w_parts, 1, 1)
        right[rows, :] = c
        hi, lo = halves(c)
        r_hi[rows, :] = hi
        r_lo[rows, :] = lo
        return squares + jnp.sum(c * c, axis=0, keepdims=True)

    squares = lax.fori_loop(0, COLS // STEP, finish, jnp.zeros((1, RANK), F32))
    sq_z[z] = squares
    n = [remote(sq_z.at[z], sq_z.at[z], at_z(d)) for d in range(1, ZS)]

    outs = []
    for g, (t, num) in enumerate(GROUPS):
        lanes = slice(128 * t, 128 * (t + num))
        ortho = mm3(w_parts, halves(whole(g)), 1, 0)
        left[lanes, :] = (ortho * F32(math.sqrt(D))).T
        o = halves(ortho)

        @pl.loop(0, COLS // STEP)
        def _(i):
            rows = pl.ds(pl.multiple_of(i * STEP, STEP), STEP)
            merged[rows, lanes] = merged[rows, lanes] - 0.5 * mm3((r_hi[rows, :], r_lo[rows, :]), o, 1, 0)

        if g == 1:
            for c in n:
                c.wait_recv()
            total = sq_z[0]
            for k in range(1, ZS):
                total = total + sq_z[k]
            sq_y[y] = total
            v = [remote(sq_y.at[y], sq_y.at[y], at_y(d)) for d in range(1, YS)]
        out = pltpu.make_async_copy(merged.at[:, lanes], newm_hbm.at[:, lanes], local.at[11 + g])
        out.start()
        outs.append(out)
    for src, dst, i in ((left, left_hbm, 14), (right, newb_hbm, 15)):
        out = pltpu.make_async_copy(src, dst, local.at[i])
        out.start()
        outs.append(out)
    for c in v:
        c.wait_recv()
    inv[...] = lax.rsqrt(((sq_y[0] + sq_y[1]) + (sq_y[2] + sq_y[3])) / F + EPS)
    out = pltpu.make_async_copy(inv, inv_hbm, local.at[16])
    out.start()
    outs.append(out)
    for c in started:
        c.wait_send()
    for out in outs:
        out.wait()


def write_out(new, left, right, inv, new_hbm, left_hbm, right_hbm, scaled, sems):
    outs = [
        pltpu.make_async_copy(new, new_hbm, sems.at[0]),
        pltpu.make_async_copy(left, left_hbm, sems.at[1]),
        pltpu.make_async_copy(scaled, right_hbm, sems.at[2]),
    ]
    outs[0].start()
    outs[1].start()
    scaled[...] = right[...] * inv[...]
    outs[2].start()
    for out in outs:
        out.wait()


COPIES = 3 * 24 + 12 + 15 + 10


def shards(momentum, activations, out_grads, basis):
    any_ = pl.BlockSpec(memory_space=pl.ANY)
    new_t, left, right, inv = pl.pallas_call(
        kernel,
        out_shape=(
            jax.ShapeDtypeStruct((COLS, ROWS), F32),
            jax.ShapeDtypeStruct((ROWS, RANK), F32),
            jax.ShapeDtypeStruct((COLS, RANK), F32),
            jax.ShapeDtypeStruct((1, RANK), F32),
        ),
        in_specs=[pl.BlockSpec(memory_space=pltpu.HBM)] * 4,
        out_specs=[any_] * 4,
        scratch_shapes=[
            pltpu.VMEM((COLS, TOKENS), BF16),
            pltpu.VMEM((TOKENS, ROWS), BF16),
            pltpu.VMEM((COLS, ROWS), F32),
            pltpu.VMEM((COLS_PAD, RANK), F32),
            pltpu.VMEM((RANK, COLS_PAD), BF16),
            pltpu.VMEM((RANK, COLS_PAD), BF16),
            pltpu.VMEM((COLS_PAD, ROWS), BF16),
            pltpu.VMEM((COLS_PAD, ROWS), BF16),
            pltpu.VMEM((5, RANK, 128), F32),
            pltpu.VMEM((2, 5, 32, 128), F32),
            pltpu.VMEM((2, 5, 32, 128), F32),
            pltpu.VMEM((2, 5, 64, 128), F32),
            pltpu.VMEM((5, 64, 128), F32),
            pltpu.VMEM((ZS - 1, 5, 8, 128), F32),
            pltpu.VMEM((5, RANK, 128), F32),
            pltpu.VMEM((3, 128, 128), F32),
            pltpu.VMEM((3, 64, 128), F32),
            pltpu.VMEM((XS, 3, 64, 128), F32),
            pltpu.VMEM((3, 128, 128), F32),
            pltpu.VMEM((2, COLS, 128), F32),
            pltpu.VMEM((COLS, 128), F32),
            pltpu.VMEM((COLS, 128), F32),
            pltpu.VMEM((216, 128), F32),
            pltpu.VMEM((4, 216, 128), F32),
            pltpu.VMEM((2, COLS, 128), F32),
            pltpu.VMEM((COLS, RANK), F32),
            pltpu.VMEM((COLS, RANK), BF16),
            pltpu.VMEM((COLS, RANK), BF16),
            pltpu.VMEM((ROWS, RANK), F32),
            pltpu.VMEM((ZS, 1, RANK), F32),
            pltpu.VMEM((YS, 1, RANK), F32),
            pltpu.VMEM((1, RANK), F32),
            pltpu.SemaphoreType.DMA((COPIES,)),
            pltpu.SemaphoreType.DMA((COPIES,)),
            pltpu.SemaphoreType.DMA((17,)),
        ],
        compiler_params=pltpu.CompilerParams(
            collective_id=0, has_side_effects=True, vmem_limit_bytes=48 * 1024 * 1024),
    )(momentum.T, activations, out_grads.T, basis)
    vmem = pl.BlockSpec(memory_space=pltpu.VMEM)
    new_t, left, right = pl.pallas_call(
        write_out,
        out_shape=(
            jax.ShapeDtypeStruct((COLS, ROWS), F32),
            jax.ShapeDtypeStruct((ROWS, RANK), F32),
            jax.ShapeDtypeStruct((COLS, RANK), F32),
        ),
        in_specs=[any_, any_, vmem, vmem],
        out_specs=[any_] * 3,
        scratch_shapes=[pltpu.VMEM((COLS, RANK), F32), pltpu.SemaphoreType.DMA((3,))],
        compiler_params=pltpu.CompilerParams(vmem_limit_bytes=8 * 1024 * 1024),
    )(new_t, left, right, inv)
    return new_t.T, left, right


def solution(mesh):
    return jax.shard_map(
        shards,
        mesh=mesh,
        in_specs=(P("row", "col"), P(None, "row"), P(None, "col"), P("col", None)),
        out_specs=(P("row", "col"), P("row", None), P("col", None)),
        check_vma=False,
    )
```

```python
import math

import jax
import jax.numpy as jnp
from jax import lax
from jax.experimental import pallas as pl
from jax.experimental.pallas import tpu as pltpu
from jax.sharding import PartitionSpec as P

D = 5120
F = 27648
EPS = 1e-06
HIGH = lax.Precision.HIGHEST
MESH = pl.DeviceIdType.MESH
F32 = jnp.float32
BF16 = jnp.bfloat16

XS, YS, ZS = 4, 4, 8
ROWS, COLS, RANK, TOKENS = 640, 864, 256, 2048
COLS_PAD = 896
STEP = 288
GROUPS = ((0, 2), (2, 2), (4, 1))
FAR_Z = (4, 3, 5, 2, 6, 1, 7)


def mm(a, b, ca, cb):
    return lax.dot_general(a, b, (((ca,), (cb,)), ((), ())), precision=HIGH, preferred_element_type=F32)


def mm16(a, b, ca, cb):
    return lax.dot_general(a, b, (((ca,), (cb,)), ((), ())), preferred_element_type=F32)


def halves(x):
    hi = x.astype(BF16)
    return hi, (x - hi.astype(F32)).astype(BF16)


def mm3(a, b, ca, cb):
    return mm16(a[0], b[0], ca, cb) + (mm16(a[0], b[1], ca, cb) + mm16(a[1], b[0], ca, cb))


def lane_of(v, c):
    return jnp.broadcast_to(v[:, c:c + 1], v.shape)

def row_of(v, r):
    return jnp.broadcast_to(v[r:r + 1, :], v.shape)

def inverse_factor_64(block):
    r64 = lax.broadcasted_iota(jnp.int32, (64, 64), 0)
    c64 = lax.broadcasted_iota(jnp.int32, (64, 64), 1)
    eye = jnp.where(r64 == c64, 1.0, 0.0).astype(jnp.float32)
    wide = jnp.concatenate([block, eye], axis=1)
    t = [wide[8 * k:8 * k + 8] for k in range(8)]
    sub = lax.broadcasted_iota(jnp.int32, (8, 128), 0)
    out = []
    for k in range(8):
        cols = [lane_of(t[k], 8 * k + c) for c in range(8)]
        e = [[row_of(cols[c], r) if r >= c else None for c in range(8)] for r in range(8)]
        rows = [row_of(t[k], r) for r in range(8)]
        rs = [None] * 8
        l = [[None] * 8 for _ in range(8)]
        for c in range(8):
            rs[c] = lax.rsqrt(e[c][c])
            rows[c] = rows[c] * rs[c]
            for r in range(c + 1, 8):
                l[r][c] = e[r][c] * rs[c]
            for r in range(c + 1, 8):
                for m in range(c + 1, r + 1):
                    e[r][m] = e[r][m] - l[r][c] * l[m][c]
                rows[r] = rows[r] - l[r][c] * rows[c]
        u = rows[0]
        for c in range(1, 8):
            u = jnp.where(sub == c, rows[c], u)
        out.append(u)
        for j in range(k + 1, 8):
            s = [lane_of(t[j], 8 * k + c) for c in range(8)]
            for c in range(8):
                s[c] = s[c] * rs[c]
                for m in range(c + 1, 8):
                    s[m] = s[m] - s[c] * l[m][c]
                t[j] = t[j] - s[c] * rows[c]
    return jnp.concatenate(out, axis=0)[:, 64:]

def joined(w11, w21, w22):
    top = jnp.concatenate([w11, jnp.zeros_like(w11)], axis=1)
    return jnp.concatenate([top, jnp.concatenate([w21, w22], axis=1)], axis=0)

def inverse_factor_step(a11, a21, a22, smaller):
    w11 = smaller(a11)
    l21 = mm(a21, w11, 1, 1)
    s = a22 - mm(l21, l21, 1, 1)
    lw = mm(l21, w11, 1, 0)
    w22 = smaller(s)
    w21 = -mm(w22, lw, 1, 0)
    return w11, w21, w22

def inverse_factor_128(a):
    return joined(*inverse_factor_step(a[:64, :64], a[64:, :64], a[64:, 64:], inverse_factor_64))


def kernel(mom_hbm, act_hbm, grad_hbm, basis_hbm, newm_hbm, left_hbm, newb_hbm, inv_hbm,
           grad, act, merged, basis, bt_hi, bt_lo, m_hi, m_lo,
           part, from_y, from_z, full,
           gram, gram_pair, gram_x, gram_all,
           coef, coef_pair, coef_sum, coef_x, coef_all,
           right, r_hi, r_lo, left, sq, inv,
           send, recv, local):
    row, col = lax.axis_index("row"), lax.axis_index("col")
    x, core = row // 2, lax.rem(row, 2)
    z, y = col // YS, lax.rem(col, YS)

    def at_y(d):
        return (row, z * YS + lax.rem(y + d, YS))

    def at_z(d):
        return (row, lax.rem(z + d, ZS) * YS + y)

    def at_x(d):
        return (lax.rem(x + d, XS) * 2 + core, col)

    other = (x * 2 + 1 - core, col)

    loads = [
        pltpu.make_async_copy(act_hbm.at[:, pl.ds(128 * t, 128 * n)], act.at[:, pl.ds(128 * t, 128 * n)], local.at[i])
        for i, (t, n) in enumerate(GROUPS)
    ]
    grad_load = [
        pltpu.make_async_copy(grad_hbm.at[pl.ds(STEP * i, STEP)], grad.at[pl.ds(STEP * i, STEP)], local.at[3 + i])
        for i in range(3)
    ]
    mom_load = [
        pltpu.make_async_copy(mom_hbm.at[pl.ds(STEP * i, STEP)], merged.at[pl.ds(STEP * i, STEP)], local.at[8 + i])
        for i in range(3)
    ]
    basis_load = pltpu.make_async_copy(basis_hbm, basis.at[pl.ds(0, COLS)], local.at[7])
    basis_load.start()
    loads[0].start()
    for i in range(2):
        grad_load[i].start()
        mom_load[i].start()

    barrier = pltpu.get_barrier_semaphore()
    same_row = [
        (row, lax.rem(z + dz, ZS) * YS + lax.rem(y + dy, YS))
        for dz in (4, 3, 5, 2, 6, 1, 7, 0) for dy in (2, 1, 3, 0) if dz or dy
    ]
    peers = same_row + [at_x(d) for d in range(1, XS)] + [other]
    for peer in peers:
        pl.semaphore_signal(barrier, inc=1, device_id=peer, device_id_type=MESH)

    count = [0]
    started = []

    def remote(src, dst, peer):
        n = count[0]
        count[0] += 1
        copy = pltpu.make_async_remote_copy(
            src_ref=src, dst_ref=dst, send_sem=send.at[n], recv_sem=recv.at[n], device_id=peer, device_id_type=MESH)
        copy.start()
        started.append(copy)
        return copy

    basis[COLS:, :] = jnp.zeros((COLS_PAD - COLS, RANK), F32)
    m_hi[COLS:, :] = jnp.zeros((COLS_PAD - COLS, ROWS), BF16)
    m_lo[COLS:, :] = jnp.zeros((COLS_PAD - COLS, ROWS), BF16)
    basis_load.wait()
    for i in range(COLS_PAD // 128):
        hi, lo = halves(basis[128 * i:128 * i + 128, :].T)
        bt_hi[:, 128 * i:128 * i + 128] = hi
        bt_lo[:, 128 * i:128 * i + 128] = lo

    def project(g):
        t, n = GROUPS[g]
        lanes = slice(128 * t, 128 * (t + n))
        loads[g].wait()

        def merge(i):
            rows = pl.ds(pl.multiple_of(i * STEP, STEP), STEP)
            m = merged[rows, lanes] + mm16(grad[rows, :], act[:, lanes], 1, 0)
            merged[rows, lanes] = m
            hi, lo = halves(m)
            m_hi[rows, lanes] = hi
            m_lo[rows, lanes] = lo

        if g == 0:
            for i in range(COLS // STEP):
                grad_load[i].wait()
                mom_load[i].wait()
                if i == 0:
                    grad_load[2].start()
                    mom_load[2].start()
                else:
                    loads[i].start()
                merge(i)
        else:
            pl.loop(0, COLS // STEP)(merge)

        p = mm3((bt_hi[...], bt_lo[...]), (m_hi[:, lanes], m_lo[:, lanes]), 1, 0)
        for k in range(n):
            part[t + k] = p[:, 128 * k:128 * k + 128]

    def span(g):
        return pl.ds(*GROUPS[g])

    def mine_y(d):
        return pl.ds(pl.multiple_of(64 * lax.rem(y + d, YS), 64), 64)

    def scatter_y(g):
        return [remote(part.at[span(g), mine_y(d)], from_y.at[d - 1, span(g)], at_y(d)) for d in (2, 1, 3)]

    def share_z(g, before):
        for c in before:
            c.wait_recv()
        t, n = GROUPS[g]
        for k in range(t, t + n):
            from_z[z, k] = (part[k, mine_y(0), :] + from_y[0, k]) + (from_y[1, k] + from_y[2, k])
        return [remote(from_z.at[z, span(g)], from_z.at[z, span(g)], at_z(d)) for d in FAR_Z]

    def gather_y(g, before):
        for c in before:
            c.wait_recv()
        t, n = GROUPS[g]
        for k in range(t, t + n):
            v = [from_z[d, k] for d in range(ZS)]
            full[k, mine_y(0), :] = ((v[0] + v[1]) + (v[2] + v[3])) + ((v[4] + v[5]) + (v[6] + v[7]))
        return [remote(full.at[span(g), mine_y(0)], full.at[span(g), mine_y(0)], at_y(d)) for d in (2, 1, 3)]

    def whole(g):
        t, n = GROUPS[g]
        return jnp.concatenate([full[k] for k in range(t, t + n)], axis=1)

    def coefficients(g):
        t, n = GROUPS[g]
        lanes = slice(128 * t, 128 * (t + n))
        p = halves(whole(g))

        @pl.loop(0, COLS // STEP)
        def _(i):
            rows = pl.ds(pl.multiple_of(i * STEP, STEP), STEP)
            c = mm3((m_hi[rows, lanes], m_lo[rows, lanes]), p, 1, 1)
            for k in range(2):
                v = c[:, 128 * k:128 * k + 128]
                coef[k, rows, :] = v if g == 0 else coef[k, rows, :] + v

    project(0)
    pl.semaphore_wait(barrier, len(peers))
    a0 = scatter_y(0)
    project(1)
    a1 = scatter_y(1)
    b0 = share_z(0, a0)
    project(2)
    a2 = scatter_y(2)
    b1 = share_z(1, a1)
    c0 = gather_y(0, b0)
    b2 = share_z(2, a2)
    for c in c0:
        c.wait_recv()
    gr = mm(whole(0), whole(0), 1, 1)
    c1 = gather_y(1, b1)
    coefficients(0)
    c2 = gather_y(2, b2)
    for c in c1:
        c.wait_recv()
    gr = gr + mm(whole(1), whole(1), 1, 1)
    coefficients(1)
    for c in c2:
        c.wait_recv()
    gr = gr + mm(whole(2), whole(2), 1, 1)

    gram[0] = gr[:128, :128]
    gram[1] = gr[128:, :128]
    gram[2] = gr[128:, 128:]
    half = pl.ds(pl.multiple_of(64 * core, 64), 64)
    other_half = pl.ds(pl.multiple_of(64 * (1 - core), 64), 64)
    e0 = remote(gram.at[pl.ds(0, 1), other_half], gram_pair.at[pl.ds(0, 1)], other)
    e1 = remote(gram.at[pl.ds(1, 2), other_half], gram_pair.at[pl.ds(1, 2)], other)
    coefficients(2)
    h = remote(coef.at[1 - core], coef_pair, other)

    def gram_over_x(b, n, before):
        before.wait_recv()
        for k in range(b, b + n):
            gram_x[x, k] = gram[k, half, :] + gram_pair[k]
        return [remote(gram_x.at[x, pl.ds(b, n)], gram_x.at[x, pl.ds(b, n)], at_x(d)) for d in range(1, XS)]

    def gram_to_pair(b, n, before):
        for c in before:
            c.wait_recv()
        for k in range(b, b + n):
            gram_all[k, half, :] = (gram_x[0, k] + gram_x[1, k]) + (gram_x[2, k] + gram_x[3, k])
        return remote(gram_all.at[pl.ds(b, n), half], gram_all.at[pl.ds(b, n), half], other)

    f0 = gram_over_x(0, 1, e0)

    def coef_rows(d):
        return pl.ds(pl.multiple_of(216 * lax.rem(x + d, XS), 216), 216)

    h.wait_recv()
    coef_sum[...] = coef[core] + coef_pair[...]
    f1 = gram_over_x(1, 2, e1)
    r = [remote(coef_sum.at[coef_rows(d)], coef_x.at[d - 1], at_x(d)) for d in range(1, XS)]
    g0 = gram_to_pair(0, 1, f0)
    g0.wait_recv()
    a11 = gram_all[0]
    w11 = inverse_factor_64(a11[:64, :64])
    l21 = mm(a11[64:, :64], w11, 1, 1)
    s = a11[64:, 64:] - mm(l21, l21, 1, 1)
    lw = mm(l21, w11, 1, 0)
    g1 = gram_to_pair(1, 2, f1)
    w22 = inverse_factor_64(s)
    wa = joined(w11, -mm(w22, lw, 1, 0), w22)
    g1.wait_recv()
    a22 = gram_all[2]
    l21 = mm(gram_all[1], wa, 1, 1)
    s = a22 - mm(l21, l21, 1, 1)
    lwa = mm(l21, wa, 1, 0)
    for c in r:
        c.wait_recv()
    coef_all[core, coef_rows(0), :] = (coef_sum[coef_rows(0), :] + coef_x[0]) + (coef_x[1] + coef_x[2])
    q = [remote(coef_all.at[core, coef_rows(0)], coef_all.at[core, coef_rows(0)], at_x(d)) for d in range(1, XS)]
    w11 = inverse_factor_64(s[:64, :64])
    l21 = mm(s[64:, :64], w11, 1, 1)
    s2 = s[64:, 64:] - mm(l21, l21, 1, 1)
    lw = mm(l21, w11, 1, 0)
    for c in q:
        c.wait_recv()
    k0 = remote(coef_all.at[core], coef_all.at[core], other)
    w22 = inverse_factor_64(s2)
    wb = joined(w11, -mm(w22, lw, 1, 0), w22)
    w = joined(wa, -mm(wb, lwa, 1, 0), wb)

    k0.wait_recv()
    w_parts = halves(w)

    def finish(i, squares):
        rows = pl.ds(pl.multiple_of(i * STEP, STEP), STEP)
        c = jnp.concatenate([coef_all[0, rows, :], coef_all[1, rows, :]], axis=1)
        c = mm3(halves(c), w_parts, 1, 1)
        right[rows, :] = c
        hi, lo = halves(c)
        r_hi[rows, :] = hi
        r_lo[rows, :] = lo
        return squares + jnp.sum(c * c, axis=0, keepdims=True)

    squares = lax.fori_loop(0, COLS // STEP, finish, jnp.zeros((1, RANK), F32))
    sq[col] = squares
    n = [remote(sq.at[col], sq.at[col], peer) for peer in same_row]

    outs = []
    for g, (t, num) in enumerate(GROUPS):
        lanes = slice(128 * t, 128 * (t + num))
        ortho = mm3(w_parts, halves(whole(g)), 1, 0)
        left[lanes, :] = (ortho * F32(math.sqrt(D))).T
        o = halves(ortho)

        @pl.loop(0, COLS // STEP)
        def _(i):
            rows = pl.ds(pl.multiple_of(i * STEP, STEP), STEP)
            merged[rows, lanes] = merged[rows, lanes] - 0.5 * mm3((r_hi[rows, :], r_lo[rows, :]), o, 1, 0)

        out = pltpu.make_async_copy(merged.at[:, lanes], newm_hbm.at[:, lanes], local.at[11 + g])
        out.start()
        outs.append(out)
    for src, dst, i in ((left, left_hbm, 14), (right, newb_hbm, 15)):
        out = pltpu.make_async_copy(src, dst, local.at[i])
        out.start()
        outs.append(out)
    for c in n:
        c.wait_recv()
    total = sq[0]
    for k in range(1, YS * ZS):
        total = total + sq[k]
    inv[...] = lax.rsqrt(total / F + EPS)
    out = pltpu.make_async_copy(inv, inv_hbm, local.at[16])
    out.start()
    outs.append(out)
    for c in started:
        c.wait_send()
    for out in outs:
        out.wait()


def write_out(new, left, right, inv, new_hbm, left_hbm, right_hbm, scaled, sems):
    outs = [
        pltpu.make_async_copy(new, new_hbm, sems.at[0]),
        pltpu.make_async_copy(left, left_hbm, sems.at[1]),
        pltpu.make_async_copy(scaled, right_hbm, sems.at[2]),
    ]
    outs[0].start()
    outs[1].start()
    scaled[...] = right[...] * inv[...]
    outs[2].start()
    for out in outs:
        out.wait()


COPIES = 3 * 13 + 10 + 8 + 31


def shards(momentum, activations, out_grads, basis):
    any_ = pl.BlockSpec(memory_space=pl.ANY)
    new_t, left, right, inv = pl.pallas_call(
        kernel,
        out_shape=(
            jax.ShapeDtypeStruct((COLS, ROWS), F32),
            jax.ShapeDtypeStruct((ROWS, RANK), F32),
            jax.ShapeDtypeStruct((COLS, RANK), F32),
            jax.ShapeDtypeStruct((1, RANK), F32),
        ),
        in_specs=[pl.BlockSpec(memory_space=pltpu.HBM)] * 4,
        out_specs=[any_] * 4,
        scratch_shapes=[
            pltpu.VMEM((COLS, TOKENS), BF16),
            pltpu.VMEM((TOKENS, ROWS), BF16),
            pltpu.VMEM((COLS, ROWS), F32),
            pltpu.VMEM((COLS_PAD, RANK), F32),
            pltpu.VMEM((RANK, COLS_PAD), BF16),
            pltpu.VMEM((RANK, COLS_PAD), BF16),
            pltpu.VMEM((COLS_PAD, ROWS), BF16),
            pltpu.VMEM((COLS_PAD, ROWS), BF16),
            pltpu.VMEM((5, RANK, 128), F32),
            pltpu.VMEM((YS - 1, 5, 64, 128), F32),
            pltpu.VMEM((ZS, 5, 64, 128), F32),
            pltpu.VMEM((5, RANK, 128), F32),
            pltpu.VMEM((3, 128, 128), F32),
            pltpu.VMEM((3, 64, 128), F32),
            pltpu.VMEM((XS, 3, 64, 128), F32),
            pltpu.VMEM((3, 128, 128), F32),
            pltpu.VMEM((2, COLS, 128), F32),
            pltpu.VMEM((COLS, 128), F32),
            pltpu.VMEM((COLS, 128), F32),
            pltpu.VMEM((XS - 1, 216, 128), F32),
            pltpu.VMEM((2, COLS, 128), F32),
            pltpu.VMEM((COLS, RANK), F32),
            pltpu.VMEM((COLS, RANK), BF16),
            pltpu.VMEM((COLS, RANK), BF16),
            pltpu.VMEM((ROWS, RANK), F32),
            pltpu.VMEM((YS * ZS, 1, RANK), F32),
            pltpu.VMEM((1, RANK), F32),
            pltpu.SemaphoreType.DMA((COPIES,)),
            pltpu.SemaphoreType.DMA((COPIES,)),
            pltpu.SemaphoreType.DMA((17,)),
        ],
        compiler_params=pltpu.CompilerParams(
            collective_id=0, has_side_effects=True, vmem_limit_bytes=48 * 1024 * 1024),
    )(momentum.T, activations, out_grads.T, basis)
    vmem = pl.BlockSpec(memory_space=pltpu.VMEM)
    new_t, left, right = pl.pallas_call(
        write_out,
        out_shape=(
            jax.ShapeDtypeStruct((COLS, ROWS), F32),
            jax.ShapeDtypeStruct((ROWS, RANK), F32),
            jax.ShapeDtypeStruct((COLS, RANK), F32),
        ),
        in_specs=[any_, any_, vmem, vmem],
        out_specs=[any_] * 3,
        scratch_shapes=[pltpu.VMEM((COLS, RANK), F32), pltpu.SemaphoreType.DMA((3,))],
        compiler_params=pltpu.CompilerParams(vmem_limit_bytes=8 * 1024 * 1024),
    )(new_t, left, right, inv)
    return new_t.T, left, right


def solution(mesh):
    return jax.shard_map(
        shards,
        mesh=mesh,
        in_specs=(P("row", "col"), P(None, "row"), P(None, "col"), P("col", None)),
        out_specs=(P("row", "col"), P("row", None), P("col", None)),
        check_vma=False,
    )
```

```python
import math

import jax
import jax.numpy as jnp
from jax import lax
from jax.experimental import pallas as pl
from jax.experimental.pallas import tpu as pltpu
from jax.sharding import PartitionSpec as P

D = 5120
F = 27648
EPS = 1e-06
HIGH = lax.Precision.HIGHEST
MESH = pl.DeviceIdType.MESH
F32 = jnp.float32
BF16 = jnp.bfloat16

XS, YS, ZS = 4, 4, 8
ROWS, COLS, RANK, TOKENS = 640, 864, 256, 2048
COLS_PAD = 896
STEP = 288
GROUPS = ((0, 2), (2, 2), (4, 1))
CHUNKS = ((0, 448), (448, 416))


def mm(a, b, ca, cb):
    return lax.dot_general(a, b, (((ca,), (cb,)), ((), ())), precision=HIGH, preferred_element_type=F32)


def mm16(a, b, ca, cb):
    return lax.dot_general(a, b, (((ca,), (cb,)), ((), ())), preferred_element_type=F32)


def halves(x):
    hi = x.astype(BF16)
    return hi, (x - hi.astype(F32)).astype(BF16)


def mm3(a, b, ca, cb):
    return mm16(a[0], b[0], ca, cb) + (mm16(a[0], b[1], ca, cb) + mm16(a[1], b[0], ca, cb))


def lane_of(v, c):
    return jnp.broadcast_to(v[:, c:c + 1], v.shape)

def row_of(v, r):
    return jnp.broadcast_to(v[r:r + 1, :], v.shape)

def inverse_factor_64(block):
    r64 = lax.broadcasted_iota(jnp.int32, (64, 64), 0)
    c64 = lax.broadcasted_iota(jnp.int32, (64, 64), 1)
    eye = jnp.where(r64 == c64, 1.0, 0.0).astype(jnp.float32)
    wide = jnp.concatenate([block, eye], axis=1)
    t = [wide[8 * k:8 * k + 8] for k in range(8)]
    sub = lax.broadcasted_iota(jnp.int32, (8, 128), 0)
    out = []
    for k in range(8):
        cols = [lane_of(t[k], 8 * k + c) for c in range(8)]
        e = [[row_of(cols[c], r) if r >= c else None for c in range(8)] for r in range(8)]
        rows = [row_of(t[k], r) for r in range(8)]
        rs = [None] * 8
        l = [[None] * 8 for _ in range(8)]
        for c in range(8):
            rs[c] = lax.rsqrt(e[c][c])
            rows[c] = rows[c] * rs[c]
            for r in range(c + 1, 8):
                l[r][c] = e[r][c] * rs[c]
            for r in range(c + 1, 8):
                for m in range(c + 1, r + 1):
                    e[r][m] = e[r][m] - l[r][c] * l[m][c]
                rows[r] = rows[r] - l[r][c] * rows[c]
        u = rows[0]
        for c in range(1, 8):
            u = jnp.where(sub == c, rows[c], u)
        out.append(u)
        for j in range(k + 1, 8):
            s = [lane_of(t[j], 8 * k + c) for c in range(8)]
            for c in range(8):
                s[c] = s[c] * rs[c]
                for m in range(c + 1, 8):
                    s[m] = s[m] - s[c] * l[m][c]
                t[j] = t[j] - s[c] * rows[c]
    return jnp.concatenate(out, axis=0)[:, 64:]

def joined(w11, w21, w22):
    top = jnp.concatenate([w11, jnp.zeros_like(w11)], axis=1)
    return jnp.concatenate([top, jnp.concatenate([w21, w22], axis=1)], axis=0)

def inverse_factor_step(a11, a21, a22, smaller):
    w11 = smaller(a11)
    l21 = mm(a21, w11, 1, 1)
    s = a22 - mm(l21, l21, 1, 1)
    lw = mm(l21, w11, 1, 0)
    w22 = smaller(s)
    w21 = -mm(w22, lw, 1, 0)
    return w11, w21, w22

def inverse_factor_128(a):
    return joined(*inverse_factor_step(a[:64, :64], a[64:, :64], a[64:, 64:], inverse_factor_64))


def kernel(mom_hbm, act_hbm, grad_hbm, basis_hbm, newm_hbm, left_hbm, newb_hbm, inv_hbm,
           grad, act, merged, basis, bt_hi, bt_lo, m_hi, m_lo,
           part, from_y, mine, from_z, full,
           gram, gram_pair, gram_x, gram_all,
           coef, coef_pair, coef_sum, coef_x, coef_all,
           right, r_hi, r_lo, left, sq_z, sq_y, inv,
           send, recv, local):
    row, col = lax.axis_index("row"), lax.axis_index("col")
    x, core = row // 2, lax.rem(row, 2)
    z, y = col // YS, lax.rem(col, YS)

    def at_y(d):
        return (row, z * YS + lax.rem(y + d, YS))

    def at_z(d):
        return (row, lax.rem(z + d, ZS) * YS + y)

    def at_x(d):
        return (lax.rem(x + d, XS) * 2 + core, col)

    other = (x * 2 + 1 - core, col)

    loads = [
        pltpu.make_async_copy(act_hbm.at[:, pl.ds(128 * t, 128 * n)], act.at[:, pl.ds(128 * t, 128 * n)], local.at[i])
        for i, (t, n) in enumerate(GROUPS)
    ]
    grad_load = [
        pltpu.make_async_copy(grad_hbm.at[pl.ds(STEP * i, STEP)], grad.at[pl.ds(STEP * i, STEP)], local.at[3 + i])
        for i in range(3)
    ]
    mom_load = pltpu.make_async_copy(mom_hbm, merged, local.at[6])
    basis_load = pltpu.make_async_copy(basis_hbm, basis.at[pl.ds(0, COLS)], local.at[7])
    basis_load.start()
    loads[0].start()
    for c in grad_load:
        c.start()
    mom_load.start()
    loads[1].start()
    loads[2].start()

    barrier = pltpu.get_barrier_semaphore()
    peers = [at_y(d) for d in range(1, YS)] + [at_z(d) for d in range(1, ZS)] + [at_x(d) for d in range(1, XS)] + [other]
    for peer in peers:
        pl.semaphore_signal(barrier, inc=1, device_id=peer, device_id_type=MESH)

    count = [0]
    started = []

    def remote(src, dst, peer):
        n = count[0]
        count[0] += 1
        copy = pltpu.make_async_remote_copy(
            src_ref=src, dst_ref=dst, send_sem=send.at[n], recv_sem=recv.at[n], device_id=peer, device_id_type=MESH)
        copy.start()
        started.append(copy)
        return copy

    basis[COLS:, :] = jnp.zeros((COLS_PAD - COLS, RANK), F32)
    m_hi[COLS:, :] = jnp.zeros((COLS_PAD - COLS, ROWS), BF16)
    m_lo[COLS:, :] = jnp.zeros((COLS_PAD - COLS, ROWS), BF16)
    basis_load.wait()
    for i in range(COLS_PAD // 128):
        hi, lo = halves(basis[128 * i:128 * i + 128, :].T)
        bt_hi[:, 128 * i:128 * i + 128] = hi
        bt_lo[:, 128 * i:128 * i + 128] = lo

    def project(g):
        t, n = GROUPS[g]
        lanes = slice(128 * t, 128 * (t + n))
        loads[g].wait()
        if g == 0:
            for c in grad_load:
                c.wait()
            mom_load.wait()

        @pl.loop(0, 2)
        def _(i):
            rows = pl.ds(pl.multiple_of(i * (COLS // 2), COLS // 2), COLS // 2)
            m = merged[rows, lanes] + mm16(grad[rows, :], act[:, lanes], 1, 0)
            merged[rows, lanes] = m
            hi, lo = halves(m)
            m_hi[rows, lanes] = hi
            m_lo[rows, lanes] = lo

        p = mm3((bt_hi[...], bt_lo[...]), (m_hi[:, lanes], m_lo[:, lanes]), 1, 0)
        for k in range(n):
            part[t + k] = p[:, 128 * k:128 * k + 128]

    def span(g):
        return pl.ds(*GROUPS[g])

    def mine_y(d):
        return pl.ds(pl.multiple_of(64 * lax.rem(y + d, YS), 64), 64)

    def mine_z(d):
        return pl.ds(pl.multiple_of(8 * lax.rem(z + d, ZS), 8), 8)

    own = pl.ds(pl.multiple_of(64 * y + 8 * z, 8), 8)

    def scatter_y(g):
        return [remote(part.at[span(g), mine_y(d)], from_y.at[d - 1, span(g)], at_y(d)) for d in range(1, YS)]

    def scatter_z(g, before):
        for c in before:
            c.wait_recv()
        t, n = GROUPS[g]
        for k in range(t, t + n):
            mine[k] = (part[k, mine_y(0), :] + from_y[0, k]) + (from_y[1, k] + from_y[2, k])
        return [remote(mine.at[span(g), mine_z(d)], from_z.at[d - 1, span(g)], at_z(d)) for d in range(1, ZS)]

    def gather_z(g, before):
        for c in before:
            c.wait_recv()
        t, n = GROUPS[g]
        for k in range(t, t + n):
            total = mine[k, mine_z(0), :]
            for d in range(ZS - 1):
                total = total + from_z[d, k]
            full[k, own, :] = total
        return [remote(full.at[span(g), own], full.at[span(g), own], at_z(d)) for d in range(1, ZS)]

    def gather_y(g, before):
        for c in before:
            c.wait_recv()
        return [remote(full.at[span(g), mine_y(0)], full.at[span(g), mine_y(0)], at_y(d)) for d in range(1, YS)]

    def whole(g):
        t, n = GROUPS[g]
        return jnp.concatenate([full[k] for k in range(t, t + n)], axis=1)

    def coefficients(g):
        t, n = GROUPS[g]
        lanes = slice(128 * t, 128 * (t + n))
        p = halves(whole(g))

        @pl.loop(0, COLS // STEP)
        def _(i):
            rows = pl.ds(pl.multiple_of(i * STEP, STEP), STEP)
            c = mm3((m_hi[rows, lanes], m_lo[rows, lanes]), p, 1, 1)
            for k in range(2):
                v = c[:, 128 * k:128 * k + 128]
                coef[k, rows, :] = v if g == 0 else coef[k, rows, :] + v

    def last_coefficients(first, size):
        t, n = GROUPS[2]
        lanes, rows = slice(128 * t, 128 * (t + n)), slice(first, first + size)
        c = mm3((m_hi[rows, lanes], m_lo[rows, lanes]), halves(whole(2)), 1, 1)
        for k in range(2):
            coef[k, rows, :] = coef[k, rows, :] + c[:, 128 * k:128 * k + 128]

    project(0)
    pl.semaphore_wait(barrier, len(peers))
    a0 = scatter_y(0)
    project(1)
    a1 = scatter_y(1)
    b0 = scatter_z(0, a0)
    project(2)
    a2 = scatter_y(2)
    b1 = scatter_z(1, a1)
    c0 = gather_z(0, b0)
    b2 = scatter_z(2, a2)
    c1 = gather_z(1, b1)
    d0 = gather_y(0, c0)
    c2 = gather_z(2, b2)
    d1 = gather_y(1, c1)
    d2 = gather_y(2, c2)
    for c in d0:
        c.wait_recv()
    gr = mm(whole(0), whole(0), 1, 1)
    coefficients(0)
    for c in d1:
        c.wait_recv()
    gr = gr + mm(whole(1), whole(1), 1, 1)
    coefficients(1)
    for c in d2:
        c.wait_recv()
    gr = gr + mm(whole(2), whole(2), 1, 1)

    gram[0] = gr[:128, :128]
    gram[1] = gr[128:, :128]
    gram[2] = gr[128:, 128:]
    half = pl.ds(pl.multiple_of(64 * core, 64), 64)
    other_half = pl.ds(pl.multiple_of(64 * (1 - core), 64), 64)
    e0 = remote(gram.at[pl.ds(0, 1), other_half], gram_pair.at[pl.ds(0, 1)], other)
    e1 = remote(gram.at[pl.ds(1, 2), other_half], gram_pair.at[pl.ds(1, 2)], other)
    def gram_over_x(b, n, before):
        before.wait_recv()
        for k in range(b, b + n):
            gram_x[x, k] = gram[k, half, :] + gram_pair[k]
        return [remote(gram_x.at[x, pl.ds(b, n)], gram_x.at[x, pl.ds(b, n)], at_x(d)) for d in range(1, XS)]

    def gram_to_pair(b, n, before):
        for c in before:
            c.wait_recv()
        for k in range(b, b + n):
            gram_all[k, half, :] = (gram_x[0, k] + gram_x[1, k]) + (gram_x[2, k] + gram_x[3, k])
        return remote(gram_all.at[pl.ds(b, n), half], gram_all.at[pl.ds(b, n), half], other)

    def chunk(c):
        return pl.ds(*CHUNKS[c])

    def quarter(c, d):
        first, size = CHUNKS[c]
        return pl.ds(pl.multiple_of(first + size // XS * lax.rem(x + d, XS), 8), size // XS)

    def coef_over_x(c, before):
        before.wait_recv()
        coef_sum[chunk(c)] = coef[core, chunk(c), :] + coef_pair[chunk(c)]
        size = CHUNKS[c][1] // XS
        return [
            remote(coef_sum.at[quarter(c, d)], coef_x.at[d - 1, pl.ds(112 * c, size)], at_x(d)) for d in (2, 1, 3)
        ]

    def coef_gather(c, before):
        for copy in before:
            copy.wait_recv()
        own, got = quarter(c, 0), pl.ds(112 * c, CHUNKS[c][1] // XS)
        coef_all[core, own, :] = (coef_sum[own, :] + coef_x[0, got, :]) + (coef_x[1, got, :] + coef_x[2, got, :])
        return [remote(coef_all.at[core, own], coef_all.at[core, own], at_x(d)) for d in (2, 1, 3)]

    def coef_to_pair(c, before):
        for copy in before:
            copy.wait_recv()
        return remote(coef_all.at[core, chunk(c)], coef_all.at[core, chunk(c)], other)

    last_coefficients(*CHUNKS[0])
    h0 = remote(coef.at[1 - core, chunk(0)], coef_pair.at[chunk(0)], other)
    f0 = gram_over_x(0, 1, e0)
    last_coefficients(*CHUNKS[1])
    h1 = remote(coef.at[1 - core, chunk(1)], coef_pair.at[chunk(1)], other)
    f1 = gram_over_x(1, 2, e1)
    r0 = coef_over_x(0, h0)
    r1 = coef_over_x(1, h1)
    g0 = gram_to_pair(0, 1, f0)
    g0.wait_recv()
    a11 = gram_all[0]
    w11 = inverse_factor_64(a11[:64, :64])
    l21 = mm(a11[64:, :64], w11, 1, 1)
    s = a11[64:, 64:] - mm(l21, l21, 1, 1)
    lw = mm(l21, w11, 1, 0)
    g1 = gram_to_pair(1, 2, f1)
    q0 = coef_gather(0, r0)
    w22 = inverse_factor_64(s)
    wa = joined(w11, -mm(w22, lw, 1, 0), w22)
    g1.wait_recv()
    q1 = coef_gather(1, r1)
    a22 = gram_all[2]
    l21 = mm(gram_all[1], wa, 1, 1)
    s = a22 - mm(l21, l21, 1, 1)
    lwa = mm(l21, wa, 1, 0)
    w11 = inverse_factor_64(s[:64, :64])
    l21 = mm(s[64:, :64], w11, 1, 1)
    s2 = s[64:, 64:] - mm(l21, l21, 1, 1)
    lw = mm(l21, w11, 1, 0)
    k0 = coef_to_pair(0, q0)
    w22 = inverse_factor_64(s2)
    k1 = coef_to_pair(1, q1)
    wb = joined(w11, -mm(w22, lw, 1, 0), w22)
    w = joined(wa, -mm(wb, lwa, 1, 0), wb)

    w_parts = halves(w)
    k0.wait_recv()
    k1.wait_recv()

    def finish(i, squares):
        rows = pl.ds(pl.multiple_of(i * STEP, STEP), STEP)
        c = jnp.concatenate([coef_all[0, rows, :], coef_all[1, rows, :]], axis=1)
        c = mm3(halves(c), w_parts, 1, 1)
        right[rows, :] = c
        hi, lo = halves(c)
        r_hi[rows, :] = hi
        r_lo[rows, :] = lo
        return squares + jnp.sum(c * c, axis=0, keepdims=True)

    squares = lax.fori_loop(0, COLS // STEP, finish, jnp.zeros((1, RANK), F32))
    sq_z[z] = squares
    n = [remote(sq_z.at[z], sq_z.at[z], at_z(d)) for d in range(1, ZS)]

    outs = []
    for g, (t, num) in enumerate(GROUPS):
        lanes = slice(128 * t, 128 * (t + num))
        ortho = mm3(w_parts, halves(whole(g)), 1, 0)
        left[lanes, :] = (ortho * F32(math.sqrt(D))).T
        o = halves(ortho)

        @pl.loop(0, COLS // STEP)
        def _(i):
            rows = pl.ds(pl.multiple_of(i * STEP, STEP), STEP)
            merged[rows, lanes] = merged[rows, lanes] - 0.5 * mm3((r_hi[rows, :], r_lo[rows, :]), o, 1, 0)

        if g == 1:
            for c in n:
                c.wait_recv()
            total = sq_z[0]
            for k in range(1, ZS):
                total = total + sq_z[k]
            sq_y[y] = total
            v = [remote(sq_y.at[y], sq_y.at[y], at_y(d)) for d in range(1, YS)]
        out = pltpu.make_async_copy(merged.at[:, lanes], newm_hbm.at[:, lanes], local.at[11 + g])
        out.start()
        outs.append(out)
    for src, dst, i in ((left, left_hbm, 14), (right, newb_hbm, 15)):
        out = pltpu.make_async_copy(src, dst, local.at[i])
        out.start()
        outs.append(out)
    for c in v:
        c.wait_recv()
    inv[...] = lax.rsqrt(((sq_y[0] + sq_y[1]) + (sq_y[2] + sq_y[3])) / F + EPS)
    out = pltpu.make_async_copy(inv, inv_hbm, local.at[16])
    out.start()
    outs.append(out)
    for c in started:
        c.wait_send()
    for out in outs:
        out.wait()


def write_out(new, left, right, inv, new_hbm, left_hbm, right_hbm, scaled, sems):
    outs = [
        pltpu.make_async_copy(new, new_hbm, sems.at[0]),
        pltpu.make_async_copy(left, left_hbm, sems.at[1]),
        pltpu.make_async_copy(scaled, right_hbm, sems.at[2]),
    ]
    outs[0].start()
    outs[1].start()
    scaled[...] = right[...] * inv[...]
    outs[2].start()
    for out in outs:
        out.wait()


COPIES = 3 * 20 + 10 + 16 + 10


def shards(momentum, activations, out_grads, basis):
    any_ = pl.BlockSpec(memory_space=pl.ANY)
    new_t, left, right, inv = pl.pallas_call(
        kernel,
        out_shape=(
            jax.ShapeDtypeStruct((COLS, ROWS), F32),
            jax.ShapeDtypeStruct((ROWS, RANK), F32),
            jax.ShapeDtypeStruct((COLS, RANK), F32),
            jax.ShapeDtypeStruct((1, RANK), F32),
        ),
        in_specs=[pl.BlockSpec(memory_space=pltpu.HBM)] * 4,
        out_specs=[any_] * 4,
        scratch_shapes=[
            pltpu.VMEM((COLS, TOKENS), BF16),
            pltpu.VMEM((TOKENS, ROWS), BF16),
            pltpu.VMEM((COLS, ROWS), F32),
            pltpu.VMEM((COLS_PAD, RANK), F32),
            pltpu.VMEM((RANK, COLS_PAD), BF16),
            pltpu.VMEM((RANK, COLS_PAD), BF16),
            pltpu.VMEM((COLS_PAD, ROWS), BF16),
            pltpu.VMEM((COLS_PAD, ROWS), BF16),
            pltpu.VMEM((5, RANK, 128), F32),
            pltpu.VMEM((YS - 1, 5, 64, 128), F32),
            pltpu.VMEM((5, 64, 128), F32),
            pltpu.VMEM((ZS - 1, 5, 8, 128), F32),
            pltpu.VMEM((5, RANK, 128), F32),
            pltpu.VMEM((3, 128, 128), F32),
            pltpu.VMEM((3, 64, 128), F32),
            pltpu.VMEM((XS, 3, 64, 128), F32),
            pltpu.VMEM((3, 128, 128), F32),
            pltpu.VMEM((2, COLS, 128), F32),
            pltpu.VMEM((COLS, 128), F32),
            pltpu.VMEM((COLS, 128), F32),
            pltpu.VMEM((XS - 1, 216, 128), F32),
            pltpu.VMEM((2, COLS, 128), F32),
            pltpu.VMEM((COLS, RANK), F32),
            pltpu.VMEM((COLS, RANK), BF16),
            pltpu.VMEM((COLS, RANK), BF16),
            pltpu.VMEM((ROWS, RANK), F32),
            pltpu.VMEM((ZS, 1, RANK), F32),
            pltpu.VMEM((YS, 1, RANK), F32),
            pltpu.VMEM((1, RANK), F32),
            pltpu.SemaphoreType.DMA((COPIES,)),
            pltpu.SemaphoreType.DMA((COPIES,)),
            pltpu.SemaphoreType.DMA((17,)),
        ],
        compiler_params=pltpu.CompilerParams(
            collective_id=0, has_side_effects=True, vmem_limit_bytes=48 * 1024 * 1024),
    )(momentum.T, activations, out_grads.T, basis)
    vmem = pl.BlockSpec(memory_space=pltpu.VMEM)
    new_t, left, right = pl.pallas_call(
        write_out,
        out_shape=(
            jax.ShapeDtypeStruct((COLS, ROWS), F32),
            jax.ShapeDtypeStruct((ROWS, RANK), F32),
            jax.ShapeDtypeStruct((COLS, RANK), F32),
        ),
        in_specs=[any_, any_, vmem, vmem],
        out_specs=[any_] * 3,
        scratch_shapes=[pltpu.VMEM((COLS, RANK), F32), pltpu.SemaphoreType.DMA((3,))],
        compiler_params=pltpu.CompilerParams(vmem_limit_bytes=8 * 1024 * 1024),
    )(new_t, left, right, inv)
    return new_t.T, left, right


def solution(mesh):
    return jax.shard_map(
        shards,
        mesh=mesh,
        in_specs=(P("row", "col"), P(None, "row"), P(None, "col"), P("col", None)),
        out_specs=(P("row", "col"), P("row", None), P("col", None)),
        check_vma=False,
    )
```

```python
import math

import jax
import jax.numpy as jnp
from jax import lax
from jax.experimental import pallas as pl
from jax.experimental.pallas import tpu as pltpu
from jax.sharding import PartitionSpec as P

D = 5120
F = 27648
EPS = 1e-06
HIGH = lax.Precision.HIGHEST
MESH = pl.DeviceIdType.MESH
F32 = jnp.float32
BF16 = jnp.bfloat16

XS, YS, ZS = 4, 4, 8
ROWS, COLS, RANK, TOKENS = 640, 864, 256, 2048
COLS_PAD = 896
STEP = 288
GROUPS = ((0, 2), (2, 2), (4, 1))
CHUNKS = ((0, 448), (448, 416))


def mm(a, b, ca, cb):
    return lax.dot_general(a, b, (((ca,), (cb,)), ((), ())), precision=HIGH, preferred_element_type=F32)


def mm16(a, b, ca, cb):
    return lax.dot_general(a, b, (((ca,), (cb,)), ((), ())), preferred_element_type=F32)


def halves(x):
    hi = x.astype(BF16)
    return hi, (x - hi.astype(F32)).astype(BF16)


def mm3(a, b, ca, cb):
    return mm16(a[0], b[0], ca, cb) + (mm16(a[0], b[1], ca, cb) + mm16(a[1], b[0], ca, cb))


def lane_of(v, c):
    return jnp.broadcast_to(v[:, c:c + 1], v.shape)

def row_of(v, r):
    return jnp.broadcast_to(v[r:r + 1, :], v.shape)

def inverse_factor_64(block, halfway=None):
    r64 = lax.broadcasted_iota(jnp.int32, (64, 64), 0)
    c64 = lax.broadcasted_iota(jnp.int32, (64, 64), 1)
    eye = jnp.where(r64 == c64, 1.0, 0.0).astype(jnp.float32)
    wide = jnp.concatenate([block, eye], axis=1)
    t = [wide[8 * k:8 * k + 8] for k in range(8)]
    sub = lax.broadcasted_iota(jnp.int32, (8, 128), 0)
    out = []
    for k in range(8):
        if k == 4 and halfway is not None:
            halfway()
        cols = [lane_of(t[k], 8 * k + c) for c in range(8)]
        e = [[row_of(cols[c], r) if r >= c else None for c in range(8)] for r in range(8)]
        rows = [row_of(t[k], r) for r in range(8)]
        rs = [None] * 8
        l = [[None] * 8 for _ in range(8)]
        for c in range(0, 8, 2):
            d = c + 1
            p, q, v = e[c][c], e[d][c], e[d][d]
            rs[c] = lax.rsqrt(p)
            rs[d] = lax.rsqrt(p * v - q * q) * (p * rs[c])
            rows[c] = rows[c] * rs[c]
            for r in range(c + 1, 8):
                l[r][c] = e[r][c] * rs[c]
            rows[d] = (rows[d] - l[d][c] * rows[c]) * rs[d]
            for r in range(d + 1, 8):
                l[r][d] = (e[r][d] - l[r][c] * l[d][c]) * rs[d]
            for r in range(d + 1, 8):
                for m in range(d + 1, r + 1):
                    e[r][m] = e[r][m] - l[r][c] * l[m][c] - l[r][d] * l[m][d]
                rows[r] = rows[r] - l[r][c] * rows[c] - l[r][d] * rows[d]
        u = rows[0]
        for c in range(1, 8):
            u = jnp.where(sub == c, rows[c], u)
        out.append(u)
        for j in range(k + 1, 8):
            s = [lane_of(t[j], 8 * k + c) for c in range(8)]
            for c in range(8):
                s[c] = s[c] * rs[c]
                for m in range(c + 1, 8):
                    s[m] = s[m] - s[c] * l[m][c]
                t[j] = t[j] - s[c] * rows[c]
    return jnp.concatenate(out, axis=0)[:, 64:]

def joined(w11, w21, w22):
    top = jnp.concatenate([w11, jnp.zeros_like(w11)], axis=1)
    return jnp.concatenate([top, jnp.concatenate([w21, w22], axis=1)], axis=0)

def inverse_factor_step(a11, a21, a22, smaller):
    w11 = smaller(a11)
    l21 = mm(a21, w11, 1, 1)
    s = a22 - mm(l21, l21, 1, 1)
    lw = mm(l21, w11, 1, 0)
    w22 = smaller(s)
    w21 = -mm(w22, lw, 1, 0)
    return w11, w21, w22

def inverse_factor_128(a):
    return joined(*inverse_factor_step(a[:64, :64], a[64:, :64], a[64:, 64:], inverse_factor_64))


def kernel(mom_hbm, act_hbm, grad_hbm, basis_hbm, newm_hbm, left_hbm, newb_hbm, inv_hbm,
           grad, act, merged, basis, bt_hi, bt_lo, m_hi, m_lo,
           part, from_y, mine, from_z, full,
           gram, gram_pair, gram_x, gram_all,
           coef, coef_pair, coef_sum, coef_x, coef_all,
           right, r_hi, r_lo, left, sq_z, sq_y, inv,
           send, recv, local):
    row, col = lax.axis_index("row"), lax.axis_index("col")
    x, core = row // 2, lax.rem(row, 2)
    z, y = col // YS, lax.rem(col, YS)

    def at_y(d):
        return (row, z * YS + lax.rem(y + d, YS))

    def at_z(d):
        return (row, lax.rem(z + d, ZS) * YS + y)

    def at_x(d):
        return (lax.rem(x + d, XS) * 2 + core, col)

    other = (x * 2 + 1 - core, col)

    loads = [
        pltpu.make_async_copy(act_hbm.at[:, pl.ds(128 * t, 128 * n)], act.at[:, pl.ds(128 * t, 128 * n)], local.at[i])
        for i, (t, n) in enumerate(GROUPS)
    ]
    grad_load = [
        pltpu.make_async_copy(grad_hbm.at[pl.ds(STEP * i, STEP)], grad.at[pl.ds(STEP * i, STEP)], local.at[3 + i])
        for i in range(3)
    ]
    mom_load = pltpu.make_async_copy(mom_hbm, merged, local.at[6])
    basis_load = pltpu.make_async_copy(basis_hbm, basis.at[pl.ds(0, COLS)], local.at[7])
    basis_load.start()
    loads[0].start()
    for c in grad_load:
        c.start()
    mom_load.start()
    loads[1].start()
    loads[2].start()

    barrier = pltpu.get_barrier_semaphore()
    peers = [at_y(d) for d in range(1, YS)] + [at_z(d) for d in range(1, ZS)] + [at_x(d) for d in range(1, XS)] + [other]
    for peer in peers:
        pl.semaphore_signal(barrier, inc=1, device_id=peer, device_id_type=MESH)

    count = [0]
    started = []

    def remote(src, dst, peer):
        n = count[0]
        count[0] += 1
        copy = pltpu.make_async_remote_copy(
            src_ref=src, dst_ref=dst, send_sem=send.at[n], recv_sem=recv.at[n], device_id=peer, device_id_type=MESH)
        copy.start()
        started.append(copy)
        return copy

    basis[COLS:, :] = jnp.zeros((COLS_PAD - COLS, RANK), F32)
    m_hi[COLS:, :] = jnp.zeros((COLS_PAD - COLS, ROWS), BF16)
    m_lo[COLS:, :] = jnp.zeros((COLS_PAD - COLS, ROWS), BF16)
    basis_load.wait()
    for i in range(COLS_PAD // 128):
        hi, lo = halves(basis[128 * i:128 * i + 128, :].T)
        bt_hi[:, 128 * i:128 * i + 128] = hi
        bt_lo[:, 128 * i:128 * i + 128] = lo

    def project(g):
        t, n = GROUPS[g]
        lanes = slice(128 * t, 128 * (t + n))
        loads[g].wait()
        if g == 0:
            for c in grad_load:
                c.wait()
            mom_load.wait()

        @pl.loop(0, 2)
        def _(i):
            rows = pl.ds(pl.multiple_of(i * (COLS // 2), COLS // 2), COLS // 2)
            m = merged[rows, lanes] + mm16(grad[rows, :], act[:, lanes], 1, 0)
            merged[rows, lanes] = m
            hi, lo = halves(m)
            m_hi[rows, lanes] = hi
            m_lo[rows, lanes] = lo

        p = mm3((bt_hi[...], bt_lo[...]), (m_hi[:, lanes], m_lo[:, lanes]), 1, 0)
        for k in range(n):
            part[t + k] = p[:, 128 * k:128 * k + 128]

    def span(g):
        return pl.ds(*GROUPS[g])

    def mine_y(d):
        return pl.ds(pl.multiple_of(64 * lax.rem(y + d, YS), 64), 64)

    def mine_z(d):
        return pl.ds(pl.multiple_of(8 * lax.rem(z + d, ZS), 8), 8)

    own = pl.ds(pl.multiple_of(64 * y + 8 * z, 8), 8)

    def scatter_y(g):
        return [remote(part.at[span(g), mine_y(d)], from_y.at[d - 1, span(g)], at_y(d)) for d in range(1, YS)]

    def scatter_z(g, before):
        for c in before:
            c.wait_recv()
        t, n = GROUPS[g]
        for k in range(t, t + n):
            mine[k] = (part[k, mine_y(0), :] + from_y[0, k]) + (from_y[1, k] + from_y[2, k])
        return [remote(mine.at[span(g), mine_z(d)], from_z.at[d - 1, span(g)], at_z(d)) for d in range(1, ZS)]

    def gather_z(g, before):
        for c in before:
            c.wait_recv()
        t, n = GROUPS[g]
        for k in range(t, t + n):
            total = mine[k, mine_z(0), :]
            for d in range(ZS - 1):
                total = total + from_z[d, k]
            full[k, own, :] = total
        return [remote(full.at[span(g), own], full.at[span(g), own], at_z(d)) for d in range(1, ZS)]

    def gather_y(g, before):
        for c in before:
            c.wait_recv()
        return [remote(full.at[span(g), mine_y(0)], full.at[span(g), mine_y(0)], at_y(d)) for d in range(1, YS)]

    def whole(g):
        t, n = GROUPS[g]
        return jnp.concatenate([full[k] for k in range(t, t + n)], axis=1)

    def coefficients(g):
        t, n = GROUPS[g]
        lanes = slice(128 * t, 128 * (t + n))
        p = halves(whole(g))

        @pl.loop(0, COLS // STEP)
        def _(i):
            rows = pl.ds(pl.multiple_of(i * STEP, STEP), STEP)
            c = mm3((m_hi[rows, lanes], m_lo[rows, lanes]), p, 1, 1)
            for k in range(2):
                v = c[:, 128 * k:128 * k + 128]
                coef[k, rows, :] = v if g == 0 else coef[k, rows, :] + v

    def last_coefficients(first, size):
        t, n = GROUPS[2]
        lanes, rows = slice(128 * t, 128 * (t + n)), slice(first, first + size)
        c = mm3((m_hi[rows, lanes], m_lo[rows, lanes]), halves(whole(2)), 1, 1)
        for k in range(2):
            coef[k, rows, :] = coef[k, rows, :] + c[:, 128 * k:128 * k + 128]

    project(0)
    pl.semaphore_wait(barrier, len(peers))
    a0 = scatter_y(0)
    project(1)
    a1 = scatter_y(1)
    b0 = scatter_z(0, a0)
    project(2)
    a2 = scatter_y(2)
    b1 = scatter_z(1, a1)
    c0 = gather_z(0, b0)
    b2 = scatter_z(2, a2)
    c1 = gather_z(1, b1)
    d0 = gather_y(0, c0)
    c2 = gather_z(2, b2)
    d1 = gather_y(1, c1)
    d2 = gather_y(2, c2)
    for c in d0:
        c.wait_recv()
    gr = mm(whole(0), whole(0), 1, 1)
    coefficients(0)
    for c in d1:
        c.wait_recv()
    gr = gr + mm(whole(1), whole(1), 1, 1)
    coefficients(1)
    for c in d2:
        c.wait_recv()
    gr = gr + mm(whole(2), whole(2), 1, 1)

    gr = gr * F32(2.0 ** -30)
    gram[0] = gr[:128, :128]
    gram[1] = gr[128:, :128]
    gram[2] = gr[128:, 128:]
    half = pl.ds(pl.multiple_of(64 * core, 64), 64)
    other_half = pl.ds(pl.multiple_of(64 * (1 - core), 64), 64)
    e0 = remote(gram.at[pl.ds(0, 1), other_half], gram_pair.at[pl.ds(0, 1)], other)
    e1 = remote(gram.at[pl.ds(1, 2), other_half], gram_pair.at[pl.ds(1, 2)], other)
    def gram_over_x(b, n, before):
        before.wait_recv()
        for k in range(b, b + n):
            gram_x[x, k] = gram[k, half, :] + gram_pair[k]
        return [remote(gram_x.at[x, pl.ds(b, n)], gram_x.at[x, pl.ds(b, n)], at_x(d)) for d in range(1, XS)]

    def gram_to_pair(b, n, before):
        for c in before:
            c.wait_recv()
        for k in range(b, b + n):
            gram_all[k, half, :] = (gram_x[0, k] + gram_x[1, k]) + (gram_x[2, k] + gram_x[3, k])
        return remote(gram_all.at[pl.ds(b, n), half], gram_all.at[pl.ds(b, n), half], other)

    def chunk(c):
        return pl.ds(*CHUNKS[c])

    def quarter(c, d):
        first, size = CHUNKS[c]
        return pl.ds(pl.multiple_of(first + size // XS * lax.rem(x + d, XS), 8), size // XS)

    def coef_over_x(c, before):
        before.wait_recv()
        coef_sum[chunk(c)] = coef[core, chunk(c), :] + coef_pair[chunk(c)]
        size = CHUNKS[c][1] // XS
        return [
            remote(coef_sum.at[quarter(c, d)], coef_x.at[d - 1, pl.ds(112 * c, size)], at_x(d)) for d in (2, 1, 3)
        ]

    def coef_gather(c, before):
        for copy in before:
            copy.wait_recv()
        own, got = quarter(c, 0), pl.ds(112 * c, CHUNKS[c][1] // XS)
        coef_all[core, own, :] = (coef_sum[own, :] + coef_x[0, got, :]) + (coef_x[1, got, :] + coef_x[2, got, :])
        return [remote(coef_all.at[core, own], coef_all.at[core, own], at_x(d)) for d in (2, 1, 3)]

    def coef_to_pair(c, before):
        for copy in before:
            copy.wait_recv()
        return remote(coef_all.at[core, chunk(c)], coef_all.at[core, chunk(c)], other)

    last_coefficients(*CHUNKS[0])
    h0 = remote(coef.at[1 - core, chunk(0)], coef_pair.at[chunk(0)], other)
    f0 = gram_over_x(0, 1, e0)
    last_coefficients(*CHUNKS[1])
    h1 = remote(coef.at[1 - core, chunk(1)], coef_pair.at[chunk(1)], other)
    f1 = gram_over_x(1, 2, e1)
    r0 = coef_over_x(0, h0)
    r1 = coef_over_x(1, h1)
    g0 = gram_to_pair(0, 1, f0)
    g0.wait_recv()
    a11 = gram_all[0]
    w11 = inverse_factor_64(a11[:64, :64])
    l21 = mm(a11[64:, :64], w11, 1, 1)
    s = a11[64:, 64:] - mm(l21, l21, 1, 1)
    lw = mm(l21, w11, 1, 0)
    g1 = gram_to_pair(1, 2, f1)
    q0 = coef_gather(0, r0)
    q1 = []
    w22 = inverse_factor_64(s, lambda: q1.extend(coef_gather(1, r1)))
    wa = joined(w11, -mm(w22, lw, 1, 0), w22)
    g1.wait_recv()
    a22 = gram_all[2]
    l21 = mm(gram_all[1], wa, 1, 1)
    s = a22 - mm(l21, l21, 1, 1)
    lwa = mm(l21, wa, 1, 0)
    w11 = inverse_factor_64(s[:64, :64])
    l21 = mm(s[64:, :64], w11, 1, 1)
    s2 = s[64:, 64:] - mm(l21, l21, 1, 1)
    lw = mm(l21, w11, 1, 0)
    k0 = coef_to_pair(0, q0)
    k1 = []
    w22 = inverse_factor_64(s2, lambda: k1.append(coef_to_pair(1, q1)))
    wb = joined(w11, -mm(w22, lw, 1, 0), w22)
    w = joined(wa, -mm(wb, lwa, 1, 0), wb)

    w_parts = halves(w * F32(2.0 ** -15))
    k0.wait_recv()
    k1[0].wait_recv()

    def finish(i, squares):
        rows = pl.ds(pl.multiple_of(i * STEP, STEP), STEP)
        c = jnp.concatenate([coef_all[0, rows, :], coef_all[1, rows, :]], axis=1)
        c = mm3(halves(c), w_parts, 1, 1)
        right[rows, :] = c
        hi, lo = halves(c)
        r_hi[rows, :] = hi
        r_lo[rows, :] = lo
        return squares + jnp.sum(c * c, axis=0, keepdims=True)

    squares = lax.fori_loop(0, COLS // STEP, finish, jnp.zeros((1, RANK), F32))
    sq_z[z] = squares
    n = [remote(sq_z.at[z], sq_z.at[z], at_z(d)) for d in range(1, ZS)]

    outs = []
    for g, (t, num) in enumerate(GROUPS):
        lanes = slice(128 * t, 128 * (t + num))
        ortho = mm3(w_parts, halves(whole(g)), 1, 0)
        left[lanes, :] = (ortho * F32(math.sqrt(D))).T
        o = halves(ortho)

        @pl.loop(0, COLS // STEP)
        def _(i):
            rows = pl.ds(pl.multiple_of(i * STEP, STEP), STEP)
            merged[rows, lanes] = merged[rows, lanes] - 0.5 * mm3((r_hi[rows, :], r_lo[rows, :]), o, 1, 0)

        if g == 1:
            for c in n:
                c.wait_recv()
            total = sq_z[0]
            for k in range(1, ZS):
                total = total + sq_z[k]
            sq_y[y] = total
            v = [remote(sq_y.at[y], sq_y.at[y], at_y(d)) for d in range(1, YS)]
        out = pltpu.make_async_copy(merged.at[:, lanes], newm_hbm.at[:, lanes], local.at[11 + g])
        out.start()
        outs.append(out)
    for src, dst, i in ((left, left_hbm, 14), (right, newb_hbm, 15)):
        out = pltpu.make_async_copy(src, dst, local.at[i])
        out.start()
        outs.append(out)
    for c in v:
        c.wait_recv()
    inv[...] = lax.rsqrt(((sq_y[0] + sq_y[1]) + (sq_y[2] + sq_y[3])) / F + EPS)
    out = pltpu.make_async_copy(inv, inv_hbm, local.at[16])
    out.start()
    outs.append(out)
    for c in started:
        c.wait_send()
    for out in outs:
        out.wait()


def write_out(new, left, right, inv, new_hbm, left_hbm, right_hbm, scaled, sems):
    outs = [
        pltpu.make_async_copy(new, new_hbm, sems.at[0]),
        pltpu.make_async_copy(left, left_hbm, sems.at[1]),
        pltpu.make_async_copy(scaled, right_hbm, sems.at[2]),
    ]
    outs[0].start()
    outs[1].start()
    scaled[...] = right[...] * inv[...]
    outs[2].start()
    for out in outs:
        out.wait()


COPIES = 3 * 20 + 10 + 16 + 10


def shards(momentum, activations, out_grads, basis):
    any_ = pl.BlockSpec(memory_space=pl.ANY)
    new_t, left, right, inv = pl.pallas_call(
        kernel,
        out_shape=(
            jax.ShapeDtypeStruct((COLS, ROWS), F32),
            jax.ShapeDtypeStruct((ROWS, RANK), F32),
            jax.ShapeDtypeStruct((COLS, RANK), F32),
            jax.ShapeDtypeStruct((1, RANK), F32),
        ),
        in_specs=[pl.BlockSpec(memory_space=pltpu.HBM)] * 4,
        out_specs=[any_] * 4,
        scratch_shapes=[
            pltpu.VMEM((COLS, TOKENS), BF16),
            pltpu.VMEM((TOKENS, ROWS), BF16),
            pltpu.VMEM((COLS, ROWS), F32),
            pltpu.VMEM((COLS_PAD, RANK), F32),
            pltpu.VMEM((RANK, COLS_PAD), BF16),
            pltpu.VMEM((RANK, COLS_PAD), BF16),
            pltpu.VMEM((COLS_PAD, ROWS), BF16),
            pltpu.VMEM((COLS_PAD, ROWS), BF16),
            pltpu.VMEM((5, RANK, 128), F32),
            pltpu.VMEM((YS - 1, 5, 64, 128), F32),
            pltpu.VMEM((5, 64, 128), F32),
            pltpu.VMEM((ZS - 1, 5, 8, 128), F32),
            pltpu.VMEM((5, RANK, 128), F32),
            pltpu.VMEM((3, 128, 128), F32),
            pltpu.VMEM((3, 64, 128), F32),
            pltpu.VMEM((XS, 3, 64, 128), F32),
            pltpu.VMEM((3, 128, 128), F32),
            pltpu.VMEM((2, COLS, 128), F32),
            pltpu.VMEM((COLS, 128), F32),
            pltpu.VMEM((COLS, 128), F32),
            pltpu.VMEM((XS - 1, 216, 128), F32),
            pltpu.VMEM((2, COLS, 128), F32),
            pltpu.VMEM((COLS, RANK), F32),
            pltpu.VMEM((COLS, RANK), BF16),
            pltpu.VMEM((COLS, RANK), BF16),
            pltpu.VMEM((ROWS, RANK), F32),
            pltpu.VMEM((ZS, 1, RANK), F32),
            pltpu.VMEM((YS, 1, RANK), F32),
            pltpu.VMEM((1, RANK), F32),
            pltpu.SemaphoreType.DMA((COPIES,)),
            pltpu.SemaphoreType.DMA((COPIES,)),
            pltpu.SemaphoreType.DMA((17,)),
        ],
        compiler_params=pltpu.CompilerParams(
            collective_id=0, has_side_effects=True, vmem_limit_bytes=48 * 1024 * 1024),
    )(momentum.T, activations, out_grads.T, basis)
    vmem = pl.BlockSpec(memory_space=pltpu.VMEM)
    new_t, left, right = pl.pallas_call(
        write_out,
        out_shape=(
            jax.ShapeDtypeStruct((COLS, ROWS), F32),
            jax.ShapeDtypeStruct((ROWS, RANK), F32),
            jax.ShapeDtypeStruct((COLS, RANK), F32),
        ),
        in_specs=[any_, any_, vmem, vmem],
        out_specs=[any_] * 3,
        scratch_shapes=[pltpu.VMEM((COLS, RANK), F32), pltpu.SemaphoreType.DMA((3,))],
        compiler_params=pltpu.CompilerParams(vmem_limit_bytes=8 * 1024 * 1024),
    )(new_t, left, right, inv)
    return new_t.T, left, right


def solution(mesh):
    return jax.shard_map(
        shards,
        mesh=mesh,
        in_specs=(P("row", "col"), P(None, "row"), P(None, "col"), P("col", None)),
        out_specs=(P("row", "col"), P("row", None), P("col", None)),
        check_vma=False,
    )
```

```python
import math

import jax
import jax.numpy as jnp
from jax import lax
from jax.experimental import pallas as pl
from jax.experimental.pallas import tpu as pltpu
from jax.sharding import PartitionSpec as P

D = 5120
F = 27648
EPS = 1e-06
HIGH = lax.Precision.HIGHEST
MESH = pl.DeviceIdType.MESH
F32 = jnp.float32
BF16 = jnp.bfloat16

XS, YS, ZS = 4, 4, 8
ROWS, COLS, RANK, TOKENS = 640, 864, 256, 2048
COLS_PAD = 896
STEP = 288
GROUPS = ((0, 2), (2, 2), (4, 1))
CHUNKS = ((0, 448), (448, 416))


def mm(a, b, ca, cb):
    return lax.dot_general(a, b, (((ca,), (cb,)), ((), ())), precision=HIGH, preferred_element_type=F32)


def mm16(a, b, ca, cb):
    return lax.dot_general(a, b, (((ca,), (cb,)), ((), ())), preferred_element_type=F32)


def halves(x):
    hi = x.astype(BF16)
    return hi, (x - hi.astype(F32)).astype(BF16)


def mm3(a, b, ca, cb):
    return mm16(a[0], b[0], ca, cb) + (mm16(a[0], b[1], ca, cb) + mm16(a[1], b[0], ca, cb))


def lane_of(v, c):
    return jnp.broadcast_to(v[:, c:c + 1], v.shape)

def row_of(v, r):
    return jnp.broadcast_to(v[r:r + 1, :], v.shape)

def inverse_factor_64(block, halfway=None):
    r64 = lax.broadcasted_iota(jnp.int32, (64, 64), 0)
    c64 = lax.broadcasted_iota(jnp.int32, (64, 64), 1)
    eye = jnp.where(r64 == c64, 1.0, 0.0).astype(jnp.float32)
    wide = jnp.concatenate([block, eye], axis=1)
    t = [wide[8 * k:8 * k + 8] for k in range(8)]
    sub = lax.broadcasted_iota(jnp.int32, (8, 128), 0)
    out = []
    for k in range(8):
        if k == 4 and halfway is not None:
            halfway()
        cols = [lane_of(t[k], 8 * k + c) for c in range(8)]
        e = [[row_of(cols[c], r) if r >= c else None for c in range(8)] for r in range(8)]
        rows = [row_of(t[k], r) for r in range(8)]
        rs = [None] * 8
        l = [[None] * 8 for _ in range(8)]
        for c in range(0, 8, 2):
            d = c + 1
            p, q, v = e[c][c], e[d][c], e[d][d]
            rs[c] = lax.rsqrt(p)
            rs[d] = lax.rsqrt(p * v - q * q) * (p * rs[c])
            rows[c] = rows[c] * rs[c]
            for r in range(c + 1, 8):
                l[r][c] = e[r][c] * rs[c]
            rows[d] = (rows[d] - l[d][c] * rows[c]) * rs[d]
            for r in range(d + 1, 8):
                l[r][d] = (e[r][d] - l[r][c] * l[d][c]) * rs[d]
            for r in range(d + 1, 8):
                for m in range(d + 1, r + 1):
                    e[r][m] = e[r][m] - l[r][c] * l[m][c] - l[r][d] * l[m][d]
                rows[r] = rows[r] - l[r][c] * rows[c] - l[r][d] * rows[d]
        u = rows[0]
        for c in range(1, 8):
            u = jnp.where(sub == c, rows[c], u)
        out.append(u)
        for j in range(k + 1, 8):
            s = [lane_of(t[j], 8 * k + c) for c in range(8)]
            for c in range(8):
                s[c] = s[c] * rs[c]
                for m in range(c + 1, 8):
                    s[m] = s[m] - s[c] * l[m][c]
                t[j] = t[j] - s[c] * rows[c]
    return jnp.concatenate(out, axis=0)[:, 64:]

def joined(w11, w21, w22):
    top = jnp.concatenate([w11, jnp.zeros_like(w11)], axis=1)
    return jnp.concatenate([top, jnp.concatenate([w21, w22], axis=1)], axis=0)

def inverse_factor_step(a11, a21, a22, smaller):
    w11 = smaller(a11)
    l21 = mm(a21, w11, 1, 1)
    s = a22 - mm(l21, l21, 1, 1)
    lw = mm(l21, w11, 1, 0)
    w22 = smaller(s)
    w21 = -mm(w22, lw, 1, 0)
    return w11, w21, w22

def inverse_factor_128(a):
    return joined(*inverse_factor_step(a[:64, :64], a[64:, :64], a[64:, 64:], inverse_factor_64))


def kernel(mom_hbm, act_hbm, grad_hbm, basis_hbm, newm_hbm, left_hbm, newb_hbm, inv_ref,
           grad, act, merged, basis, bt_hi, bt_lo, m_hi, m_lo,
           part, from_y, mine, from_z, full,
           gram, gram_pair, gram_x, gram_all,
           coef, coef_pair, coef_sum, coef_x, coef_all,
           right, r_hi, r_lo, left, sq_z, sq_y,
           send, recv, local):
    row, col = lax.axis_index("row"), lax.axis_index("col")
    x, core = row // 2, lax.rem(row, 2)
    z, y = col // YS, lax.rem(col, YS)

    def at_y(d):
        return (row, z * YS + lax.rem(y + d, YS))

    def at_z(d):
        return (row, lax.rem(z + d, ZS) * YS + y)

    def at_x(d):
        return (lax.rem(x + d, XS) * 2 + core, col)

    other = (x * 2 + 1 - core, col)

    loads = [
        pltpu.make_async_copy(act_hbm.at[:, pl.ds(128 * t, 128 * n)], act.at[:, pl.ds(128 * t, 128 * n)], local.at[i])
        for i, (t, n) in enumerate(GROUPS)
    ]
    grad_load = [
        pltpu.make_async_copy(grad_hbm.at[pl.ds(STEP * i, STEP)], grad.at[pl.ds(STEP * i, STEP)], local.at[3 + i])
        for i in range(3)
    ]
    mom_load = pltpu.make_async_copy(mom_hbm, merged, local.at[6])
    basis_load = pltpu.make_async_copy(basis_hbm, basis.at[pl.ds(0, COLS)], local.at[7])
    basis_load.start()
    loads[0].start()
    for c in grad_load:
        c.start()
    mom_load.start()
    loads[1].start()
    loads[2].start()

    barrier = pltpu.get_barrier_semaphore()
    peers = [at_y(d) for d in range(1, YS)] + [at_z(d) for d in range(1, ZS)] + [at_x(d) for d in range(1, XS)] + [other]
    for peer in peers:
        pl.semaphore_signal(barrier, inc=1, device_id=peer, device_id_type=MESH)

    count = [0]
    started = []

    def remote(src, dst, peer):
        n = count[0]
        count[0] += 1
        copy = pltpu.make_async_remote_copy(
            src_ref=src, dst_ref=dst, send_sem=send.at[n], recv_sem=recv.at[n], device_id=peer, device_id_type=MESH)
        copy.start()
        started.append(copy)
        return copy

    basis[COLS:, :] = jnp.zeros((COLS_PAD - COLS, RANK), F32)
    m_hi[COLS:, :] = jnp.zeros((COLS_PAD - COLS, ROWS), BF16)
    m_lo[COLS:, :] = jnp.zeros((COLS_PAD - COLS, ROWS), BF16)
    basis_load.wait()
    for i in range(COLS_PAD // 128):
        hi, lo = halves(basis[128 * i:128 * i + 128, :].T)
        bt_hi[:, 128 * i:128 * i + 128] = hi
        bt_lo[:, 128 * i:128 * i + 128] = lo

    def project(g):
        t, n = GROUPS[g]
        lanes = slice(128 * t, 128 * (t + n))
        loads[g].wait()
        if g == 0:
            for c in grad_load:
                c.wait()
            mom_load.wait()

        @pl.loop(0, 2)
        def _(i):
            rows = pl.ds(pl.multiple_of(i * (COLS // 2), COLS // 2), COLS // 2)
            m = merged[rows, lanes] + mm16(grad[rows, :], act[:, lanes], 1, 0)
            merged[rows, lanes] = m
            hi, lo = halves(m)
            m_hi[rows, lanes] = hi
            m_lo[rows, lanes] = lo

        p = mm3((bt_hi[...], bt_lo[...]), (m_hi[:, lanes], m_lo[:, lanes]), 1, 0)
        for k in range(n):
            part[t + k] = p[:, 128 * k:128 * k + 128]

    def span(g):
        return pl.ds(*GROUPS[g])

    def mine_y(d):
        return pl.ds(pl.multiple_of(64 * lax.rem(y + d, YS), 64), 64)

    def mine_z(d):
        return pl.ds(pl.multiple_of(8 * lax.rem(z + d, ZS), 8), 8)

    own = pl.ds(pl.multiple_of(64 * y + 8 * z, 8), 8)

    def scatter_y(g):
        return [remote(part.at[span(g), mine_y(d)], from_y.at[d - 1, span(g)], at_y(d)) for d in range(1, YS)]

    def scatter_z(g, before):
        for c in before:
            c.wait_recv()
        t, n = GROUPS[g]
        for k in range(t, t + n):
            mine[k] = (part[k, mine_y(0), :] + from_y[0, k]) + (from_y[1, k] + from_y[2, k])
        return [remote(mine.at[span(g), mine_z(d)], from_z.at[d - 1, span(g)], at_z(d)) for d in range(1, ZS)]

    def gather_z(g, before):
        for c in before:
            c.wait_recv()
        t, n = GROUPS[g]
        for k in range(t, t + n):
            total = mine[k, mine_z(0), :]
            for d in range(ZS - 1):
                total = total + from_z[d, k]
            full[k, own, :] = total
        return [remote(full.at[span(g), own], full.at[span(g), own], at_z(d)) for d in range(1, ZS)]

    def gather_y(g, before):
        for c in before:
            c.wait_recv()
        return [remote(full.at[span(g), mine_y(0)], full.at[span(g), mine_y(0)], at_y(d)) for d in range(1, YS)]

    def whole(g):
        t, n = GROUPS[g]
        return jnp.concatenate([full[k] for k in range(t, t + n)], axis=1)

    def coefficients(g):
        t, n = GROUPS[g]
        lanes = slice(128 * t, 128 * (t + n))
        p = halves(whole(g))

        @pl.loop(0, COLS // STEP)
        def _(i):
            rows = pl.ds(pl.multiple_of(i * STEP, STEP), STEP)
            c = mm3((m_hi[rows, lanes], m_lo[rows, lanes]), p, 1, 1)
            for k in range(2):
                v = c[:, 128 * k:128 * k + 128]
                coef[k, rows, :] = v if g == 0 else coef[k, rows, :] + v

    def last_coefficients(first, size):
        t, n = GROUPS[2]
        lanes, rows = slice(128 * t, 128 * (t + n)), slice(first, first + size)
        c = mm3((m_hi[rows, lanes], m_lo[rows, lanes]), halves(whole(2)), 1, 1)
        for k in range(2):
            coef[k, rows, :] = coef[k, rows, :] + c[:, 128 * k:128 * k + 128]

    project(0)
    pl.semaphore_wait(barrier, len(peers))
    a0 = scatter_y(0)
    project(1)
    a1 = scatter_y(1)
    b0 = scatter_z(0, a0)
    project(2)
    a2 = scatter_y(2)
    b1 = scatter_z(1, a1)
    c0 = gather_z(0, b0)
    b2 = scatter_z(2, a2)
    c1 = gather_z(1, b1)
    d0 = gather_y(0, c0)
    c2 = gather_z(2, b2)
    d1 = gather_y(1, c1)
    d2 = gather_y(2, c2)
    for c in d0:
        c.wait_recv()
    gr = mm(whole(0), whole(0), 1, 1)
    coefficients(0)
    for c in d1:
        c.wait_recv()
    gr = gr + mm(whole(1), whole(1), 1, 1)
    coefficients(1)
    for c in d2:
        c.wait_recv()
    gr = gr + mm(whole(2), whole(2), 1, 1)

    gr = gr * F32(2.0 ** -30)
    gram[0] = gr[:128, :128]
    gram[1] = gr[128:, :128]
    gram[2] = gr[128:, 128:]
    half = pl.ds(pl.multiple_of(64 * core, 64), 64)
    other_half = pl.ds(pl.multiple_of(64 * (1 - core), 64), 64)
    e0 = remote(gram.at[pl.ds(0, 1), other_half], gram_pair.at[pl.ds(0, 1)], other)
    e1 = remote(gram.at[pl.ds(1, 2), other_half], gram_pair.at[pl.ds(1, 2)], other)
    def gram_over_x(b, n, before):
        before.wait_recv()
        for k in range(b, b + n):
            gram_x[x, k] = gram[k, half, :] + gram_pair[k]
        return [remote(gram_x.at[x, pl.ds(b, n)], gram_x.at[x, pl.ds(b, n)], at_x(d)) for d in range(1, XS)]

    def gram_to_pair(b, n, before):
        for c in before:
            c.wait_recv()
        for k in range(b, b + n):
            gram_all[k, half, :] = (gram_x[0, k] + gram_x[1, k]) + (gram_x[2, k] + gram_x[3, k])
        return remote(gram_all.at[pl.ds(b, n), half], gram_all.at[pl.ds(b, n), half], other)

    def chunk(c):
        return pl.ds(*CHUNKS[c])

    def quarter(c, d):
        first, size = CHUNKS[c]
        return pl.ds(pl.multiple_of(first + size // XS * lax.rem(x + d, XS), 8), size // XS)

    def coef_over_x(c, before):
        before.wait_recv()
        coef_sum[chunk(c)] = coef[core, chunk(c), :] + coef_pair[chunk(c)]
        size = CHUNKS[c][1] // XS
        return [
            remote(coef_sum.at[quarter(c, d)], coef_x.at[d - 1, pl.ds(112 * c, size)], at_x(d)) for d in (2, 1, 3)
        ]

    def coef_gather(c, before):
        for copy in before:
            copy.wait_recv()
        own, got = quarter(c, 0), pl.ds(112 * c, CHUNKS[c][1] // XS)
        coef_all[core, own, :] = (coef_sum[own, :] + coef_x[0, got, :]) + (coef_x[1, got, :] + coef_x[2, got, :])
        return [remote(coef_all.at[core, own], coef_all.at[core, own], at_x(d)) for d in (2, 1, 3)]

    def coef_to_pair(c, before):
        for copy in before:
            copy.wait_recv()
        return remote(coef_all.at[core, chunk(c)], coef_all.at[core, chunk(c)], other)

    last_coefficients(*CHUNKS[0])
    h0 = remote(coef.at[1 - core, chunk(0)], coef_pair.at[chunk(0)], other)
    f0 = gram_over_x(0, 1, e0)
    last_coefficients(*CHUNKS[1])
    h1 = remote(coef.at[1 - core, chunk(1)], coef_pair.at[chunk(1)], other)
    r0 = coef_over_x(0, h0)
    f1 = gram_over_x(1, 2, e1)
    r1 = coef_over_x(1, h1)
    g0 = gram_to_pair(0, 1, f0)
    g0.wait_recv()
    a11 = gram_all[0]
    w11 = inverse_factor_64(a11[:64, :64])
    l21 = mm(a11[64:, :64], w11, 1, 1)
    s = a11[64:, 64:] - mm(l21, l21, 1, 1)
    lw = mm(l21, w11, 1, 0)
    g1 = gram_to_pair(1, 2, f1)
    q0 = coef_gather(0, r0)
    q1 = []
    w22 = inverse_factor_64(s, lambda: q1.extend(coef_gather(1, r1)))
    wa = joined(w11, -mm(w22, lw, 1, 0), w22)
    g1.wait_recv()
    a22 = gram_all[2]
    l21 = mm(gram_all[1], wa, 1, 1)
    s = a22 - mm(l21, l21, 1, 1)
    lwa = mm(l21, wa, 1, 0)
    w11 = inverse_factor_64(s[:64, :64])
    l21 = mm(s[64:, :64], w11, 1, 1)
    s2 = s[64:, 64:] - mm(l21, l21, 1, 1)
    lw = mm(l21, w11, 1, 0)
    k0 = coef_to_pair(0, q0)
    k1 = []
    w22 = inverse_factor_64(s2, lambda: k1.append(coef_to_pair(1, q1)))
    wb = joined(w11, -mm(w22, lw, 1, 0), w22)
    w = joined(wa, -mm(wb, lwa, 1, 0), wb)

    w_parts = halves(w * F32(2.0 ** -15))
    k0.wait_recv()
    k1[0].wait_recv()

    def finish(i, squares):
        rows = pl.ds(pl.multiple_of(i * (COLS // 2), COLS // 2), COLS // 2)
        c = jnp.concatenate([coef_all[0, rows, :], coef_all[1, rows, :]], axis=1)
        c = mm3(halves(c), w_parts, 1, 1)
        right[rows, :] = c
        hi, lo = halves(c)
        r_hi[rows, :] = hi
        r_lo[rows, :] = lo
        return squares + jnp.sum(c * c, axis=0, keepdims=True)

    squares = lax.fori_loop(0, 2, finish, jnp.zeros((1, RANK), F32))
    sq_z[z] = squares
    n = [remote(sq_z.at[z], sq_z.at[z], at_z(d)) for d in range(1, ZS)]

    outs = []
    for g, (t, num) in enumerate(GROUPS):
        lanes = slice(128 * t, 128 * (t + num))
        ortho = mm3(w_parts, halves(whole(g)), 1, 0)
        left[lanes, :] = (ortho * F32(math.sqrt(D))).T
        o = halves(ortho)

        @pl.loop(0, COLS // STEP)
        def _(i):
            rows = pl.ds(pl.multiple_of(i * STEP, STEP), STEP)
            merged[rows, lanes] = merged[rows, lanes] - 0.5 * mm3((r_hi[rows, :], r_lo[rows, :]), o, 1, 0)

        if g == 1:
            for c in n:
                c.wait_recv()
            total = sq_z[0]
            for k in range(1, ZS):
                total = total + sq_z[k]
            sq_y[y] = total
            v = [remote(sq_y.at[y], sq_y.at[y], at_y(d)) for d in range(1, YS)]
        out = pltpu.make_async_copy(merged.at[:, lanes], newm_hbm.at[:, lanes], local.at[11 + g])
        out.start()
        outs.append(out)
    for src, dst, i in ((left, left_hbm, 14), (right, newb_hbm, 15)):
        out = pltpu.make_async_copy(src, dst, local.at[i])
        out.start()
        outs.append(out)
    for c in v:
        c.wait_recv()
    inv_ref[...] = lax.rsqrt(((sq_y[0] + sq_y[1]) + (sq_y[2] + sq_y[3])) / F + EPS)
    for c in started:
        c.wait_send()
    for out in outs:
        out.wait()


def write_out(new, left, right, inv, new_hbm, left_hbm, right_hbm, scaled, sems):
    outs = [
        pltpu.make_async_copy(new, new_hbm, sems.at[0]),
        pltpu.make_async_copy(left, left_hbm, sems.at[1]),
        pltpu.make_async_copy(scaled, right_hbm, sems.at[2]),
    ]
    outs[0].start()
    outs[1].start()
    scaled[...] = right[...] * inv[...]
    outs[2].start()
    for out in outs:
        out.wait()


COPIES = 3 * 20 + 10 + 16 + 10


def shards(momentum, activations, out_grads, basis):
    any_ = pl.BlockSpec(memory_space=pl.ANY)
    new_t, left, right, inv = pl.pallas_call(
        kernel,
        out_shape=(
            jax.ShapeDtypeStruct((COLS, ROWS), F32),
            jax.ShapeDtypeStruct((ROWS, RANK), F32),
            jax.ShapeDtypeStruct((COLS, RANK), F32),
            jax.ShapeDtypeStruct((1, RANK), F32),
        ),
        in_specs=[pl.BlockSpec(memory_space=pltpu.HBM)] * 4,
        out_specs=[any_] * 3 + [pl.BlockSpec(memory_space=pltpu.VMEM)],
        scratch_shapes=[
            pltpu.VMEM((COLS, TOKENS), BF16),
            pltpu.VMEM((TOKENS, ROWS), BF16),
            pltpu.VMEM((COLS, ROWS), F32),
            pltpu.VMEM((COLS_PAD, RANK), F32),
            pltpu.VMEM((RANK, COLS_PAD), BF16),
            pltpu.VMEM((RANK, COLS_PAD), BF16),
            pltpu.VMEM((COLS_PAD, ROWS), BF16),
            pltpu.VMEM((COLS_PAD, ROWS), BF16),
            pltpu.VMEM((5, RANK, 128), F32),
            pltpu.VMEM((YS - 1, 5, 64, 128), F32),
            pltpu.VMEM((5, 64, 128), F32),
            pltpu.VMEM((ZS - 1, 5, 8, 128), F32),
            pltpu.VMEM((5, RANK, 128), F32),
            pltpu.VMEM((3, 128, 128), F32),
            pltpu.VMEM((3, 64, 128), F32),
            pltpu.VMEM((XS, 3, 64, 128), F32),
            pltpu.VMEM((3, 128, 128), F32),
            pltpu.VMEM((2, COLS, 128), F32),
            pltpu.VMEM((COLS, 128), F32),
            pltpu.VMEM((COLS, 128), F32),
            pltpu.VMEM((XS - 1, 216, 128), F32),
            pltpu.VMEM((2, COLS, 128), F32),
            pltpu.VMEM((COLS, RANK), F32),
            pltpu.VMEM((COLS, RANK), BF16),
            pltpu.VMEM((COLS, RANK), BF16),
            pltpu.VMEM((ROWS, RANK), F32),
            pltpu.VMEM((ZS, 1, RANK), F32),
            pltpu.VMEM((YS, 1, RANK), F32),
            pltpu.SemaphoreType.DMA((COPIES,)),
            pltpu.SemaphoreType.DMA((COPIES,)),
            pltpu.SemaphoreType.DMA((17,)),
        ],
        compiler_params=pltpu.CompilerParams(
            collective_id=0, has_side_effects=True, vmem_limit_bytes=48 * 1024 * 1024),
    )(momentum.T, activations, out_grads.T, basis)
    vmem = pl.BlockSpec(memory_space=pltpu.VMEM)
    new_t, left, right = pl.pallas_call(
        write_out,
        out_shape=(
            jax.ShapeDtypeStruct((COLS, ROWS), F32),
            jax.ShapeDtypeStruct((ROWS, RANK), F32),
            jax.ShapeDtypeStruct((COLS, RANK), F32),
        ),
        in_specs=[any_, any_, vmem, vmem],
        out_specs=[any_] * 3,
        scratch_shapes=[pltpu.VMEM((COLS, RANK), F32), pltpu.SemaphoreType.DMA((3,))],
        compiler_params=pltpu.CompilerParams(vmem_limit_bytes=8 * 1024 * 1024),
    )(new_t, left, right, inv)
    return new_t.T, left, right


def solution(mesh):
    return jax.shard_map(
        shards,
        mesh=mesh,
        in_specs=(P("row", "col"), P(None, "row"), P(None, "col"), P("col", None)),
        out_specs=(P("row", "col"), P("row", None), P("col", None)),
        check_vma=False,
    )
```
